256 devices in a mesh: req: 8 (over z_hi, x), tile: 16 (over z_lo, y), tp: 2 (over core).
Axes of the slice: x: 4, y: 4, z: 8 (z_hi: 2, z_lo: 4; z = z_hi * 4 + z_lo), core: 2. Of those that a mesh axis runs over, the one named last changes fastest.
Arguments:
- image_qkv: bfloat16 [128, 144, 3, 2048], P(('req', 'tile'), None, None, 'tp'), parts along dimension 0, may hold values from -6 to 6
- text_kv: bfloat16 [4096, 2, 2048], P(('req', 'tile'), None, 'tp'), parts along dimension 0, may hold values from -6 to 6
- q_gain: float32 [128], replicated, may hold values from 0.7 to 5
- k_gain: float32 [128], replicated, may hold values from 0.7 to 5
- out_weight: bfloat16 [2048, 3072], P('tp'), may hold values from -0.125 to 0.125
- hidden: bfloat16 [128, 144, 3072], P(('req', 'tile')), parts along dimension 0, may hold values from -6 to 6
- mlp_term: bfloat16 [128, 144, 3072], P(('req', 'tile')), parts along dimension 0, may hold values from -3 to 3
- gate: float32 [24576], P('req'), parts along dimension 0, may hold values from -4 to 4
- final_shift: float32 [24576], P('req'), parts along dimension 0, may hold values from -3 to 3
- final_scale: float32 [24576], P('req'), parts along dimension 0, may hold values from -3 to 3
- final_weight: bfloat16 [3072, 64], replicated, may hold values from -0.109375 to 0.109375
- final_bias: float32 [64], replicated, may hold values from -3 to 3
- latent: float32 [128, 144, 64], P(('req', 'tile')), parts along dimension 0, may hold values from -6 to 6
- image_size: int32 [16], P('req'), parts along dimension 0, may hold values from 24 to 48, as said below
- text_len: int32 [8], P('req'), parts along dimension 0, may hold values from 64 to 512
- timestep: int32 [8], P('req'), parts along dimension 0, may hold values from 0 to 27
Outputs:
- velocity: float32 [128, 144, 64], P(('req', 'tile')), parts along dimension 0
- latent_next: float32 [128, 144, 64], P(('req', 'tile')), parts along dimension 0
The draws below stay inside these ranges and needn't reach their ends.
There are 8 independent parts, one for each index of `req`. The reference program is written for one: setup_inputs(seed, part) draws one part's arguments, and reference() takes and returns one part's arrays. A program takes and returns all parts, laid end to end along the dimension named above; an argument that names none is the same for every part. Nothing has to cross between parts.
Inputs may be any that keep to these rules, and one draw needn't show every extreme that they name: The larger of image_size[0] and image_size[1] equals 48.
All inputs are finite; a program needn't handle non-finite values.
Results may differ from the reference program's by a relative error of at most 0.014.
The reference program's roundings to bfloat16 on the way count: a program that leaves them out, or rounds other values in their place, can miss the bound.
Values may be sent and summed in bfloat16 or wider, within the bound.
No kernel may reach another device: no remote copies, remote signals or barrier semaphores. Data moves between devices by JAX's collectives and lax.ppermute only.
A program may use at most 128 MiB of HBM per device.

```python
import math
import jax
import jax.numpy as jnp
from jax import lax

D = 3072
HEADS = 16
HEAD = 128
LAT = 64
TEXT = 512
STEPS = 28
CANVAS = 48
TILES = 16
GRID_X = 4
TILE_H = 12
TILE_W = 12
PIX = 144


def pair_draw(key):
    base = jax.random.fold_in(key, 7001)
    image_part = jax.random.normal(jax.random.fold_in(base, 2), (TILES, PIX, 3, HEADS * HEAD))
    text_part = jax.random.normal(jax.random.fold_in(base, 4), (TEXT, 2, HEADS * HEAD))
    image_part = jnp.clip(image_part, -6.0, 6.0)
    text_part = jnp.clip(text_part, -6.0, 6.0)
    return (image_part.astype(jnp.bfloat16), text_part.astype(jnp.bfloat16))


def draw_image_qkv(key, part):
    return pair_draw(key)[0]


def draw_text_kv(key, part):
    return pair_draw(key)[1]


def gain_draw(key, salt):
    base = jax.random.fold_in(key, salt)
    spread = jnp.exp(jax.random.uniform(base, (HEAD,), minval=math.log(0.7), maxval=math.log(2.8)))
    return spread.astype(jnp.float32)


def draw_q_gain(key, part):
    return gain_draw(key, 8101)


def draw_k_gain(key, part):
    return gain_draw(key, 8202)


def draw_image_size(key, part):
    shorter = jax.random.randint(jax.random.fold_in(key, 9101), (), CANVAS // 2, CANVAS + 1)
    flipped = jax.random.randint(jax.random.fold_in(key, 9102), (), 0, 2)
    longer = jnp.int32(CANVAS)
    return jnp.stack([jnp.where(flipped == 1, longer, shorter), jnp.where(flipped == 1, shorter, longer)]).astype(jnp.int32)


def block_levels(stream_key, extent, shards, low, largest):
    factor_of = 1.0
    for axis_at, shards_of in shards:
        draws = jax.random.uniform(jax.random.fold_in(jax.random.fold_in(stream_key, 6), axis_at), (shards_of,), jnp.float32, low / len(shards), largest / len(shards))
        factor_of = factor_of * jnp.repeat(jnp.exp(draws), extent[axis_at] // shards_of).reshape((-1,) + (1,) * (len(extent) - 1 - axis_at))
    return factor_of


def gaussian(rng, shape, width, bound, split=(), kind=jnp.bfloat16):
    drawn = jax.random.normal(rng, shape, jnp.float32) * width
    if len(split) > 0:
        drawn = block_levels(rng, shape, split, -0.22, 0.18) * drawn
    return jnp.clip(drawn, min=-bound, max=bound).astype(kind)


def setup_inputs(seed: int = 0, part: int = 0) -> dict:
    streams_of = jax.random.split(jax.random.key(seed), 17)
    part_splits = jax.random.split(jax.random.fold_in(streams_of[16], part), 17)
    image_qkv = draw_image_qkv(jax.random.fold_in(jax.random.fold_in(streams_of[16], part), 71), part)
    text_kv = draw_text_kv(jax.random.fold_in(jax.random.fold_in(streams_of[16], part), 71), part)
    q_gain = draw_q_gain(jax.random.fold_in(streams_of[16], 71), part)
    k_gain = draw_k_gain(jax.random.fold_in(streams_of[16], 71), part)
    out_weight = gaussian(streams_of[4], (HEADS * HEAD, D), (HEADS * HEAD) ** -0.5, 0.125, ((0, 2),))
    hidden = gaussian(part_splits[5], (TILES, PIX, D), 1.0, 6.0, ((0, 16),))
    mlp_term = gaussian(part_splits[6], (TILES, PIX, D), 0.5, 3.0, ((0, 16),))
    gate = gaussian(part_splits[7], (D,), 1.0, 4.0, (), jnp.float32)
    final_shift = gaussian(part_splits[8], (D,), 0.5, 3.0, (), jnp.float32)
    final_scale = gaussian(part_splits[9], (D,), 0.5, 3.0, (), jnp.float32)
    final_weight = gaussian(streams_of[10], (D, LAT), D ** -0.5, 0.109375)
    final_bias = gaussian(streams_of[11], (LAT,), 0.5, 3.0, (), jnp.float32)
    latent = gaussian(part_splits[12], (TILES, PIX, LAT), 1.0, 6.0, ((0, 16),), jnp.float32)
    image_size = draw_image_size(jax.random.fold_in(jax.random.fold_in(streams_of[16], part), 71), part)
    text_len = jax.random.randint(part_splits[14], (1,), TEXT // 8, TEXT + 1).astype(jnp.int32)
    timestep = jax.random.randint(part_splits[15], (1,), 0, STEPS).astype(jnp.int32)
    return dict(image_qkv=image_qkv, text_kv=text_kv, q_gain=q_gain, k_gain=k_gain, out_weight=out_weight, hidden=hidden, mlp_term=mlp_term, gate=gate, final_shift=final_shift, final_scale=final_scale, final_weight=final_weight, final_bias=final_bias, latent=latent, image_size=image_size, text_len=text_len, timestep=timestep)


def angle_table(row_pos, col_pos, head_size):
    first_part = head_size // 8
    side_dims = (head_size - first_part) // 2
    side_index = jnp.arange(side_dims // 2, dtype=jnp.float32)
    frequency = jnp.power(10000.0, -2.0 * side_index / side_dims)
    still = jnp.zeros(row_pos.shape + (first_part // 2,), jnp.float32)
    return jnp.concatenate([still, row_pos[..., None] * frequency, col_pos[..., None] * frequency], axis=-1)

def norm_rope(vectors, gain_vector, angles):
    values_wide = vectors.astype(jnp.float32)
    scaled = values_wide * lax.rsqrt(lax.optimization_barrier(jnp.mean(values_wide * values_wide, axis=-1, keepdims=True)) + 1e-06) * gain_vector
    paired = scaled.reshape(scaled.shape[:-1] + (scaled.shape[-1] // 2, 2))
    cosine = jnp.cos(angles)[:, None, :]
    sine = jnp.sin(angles)[:, None, :]
    first_part = paired[..., 0]
    second_part = paired[..., 1]
    rotated = jnp.stack([first_part * cosine - second_part * sine, first_part * sine + second_part * cosine], axis=-1)
    return rotated.reshape(scaled.shape).astype(jnp.bfloat16)

def euler_step(image_size, timestep):
    area = (image_size[0] * image_size[1]).astype(jnp.float32)
    shift_factor = jnp.exp(0.5 + 0.65 * (area - 256.0) / 3840.0)
    now_time = 1.0 - timestep[0].astype(jnp.float32) / STEPS
    next_time = 1.0 - (timestep[0] + 1).astype(jnp.float32) / STEPS

    def sigma_of(moment):
        return shift_factor * moment / (shift_factor * moment + 1.0 - moment)
    return sigma_of(next_time) - sigma_of(now_time)

def reference(image_qkv, text_kv, q_gain, k_gain, out_weight, hidden, mlp_term, gate, final_shift, final_scale, final_weight, final_bias, latent, image_size, text_len, timestep):
    tile_number = jnp.arange(TILES, dtype=jnp.int32)[:, None]
    local_index = jnp.arange(PIX, dtype=jnp.int32)[None, :]
    row_pos = (tile_number // GRID_X * TILE_H + local_index // TILE_W).reshape(-1)
    col_pos = (tile_number % GRID_X * TILE_W + local_index % TILE_W).reshape(-1)
    patch_live = (row_pos < image_size[0]) & (col_pos < image_size[1])
    text_live = jnp.arange(TEXT, dtype=jnp.int32) < text_len[0]
    key_live = jnp.concatenate([patch_live, text_live])
    angles = angle_table(row_pos.astype(jnp.float32), col_pos.astype(jnp.float32), HEAD)
    text_angles = jnp.zeros((TEXT, HEAD // 2), jnp.float32)
    triple = image_qkv.reshape(TILES * PIX, 3, HEADS, HEAD)
    text_pair = text_kv.reshape(TEXT, 2, HEADS, HEAD)
    queries = norm_rope(triple[:, 0], q_gain, angles)
    keys_all = jnp.concatenate([norm_rope(triple[:, 1], k_gain, angles), norm_rope(text_pair[:, 0], k_gain, text_angles)], axis=0)
    values_all = jnp.concatenate([triple[:, 2], text_pair[:, 1]], axis=0)
    scale_factor = HEAD ** (-0.5)

    def one_head(operands):
        head_queries, head_keys, head_values = operands
        scores = jnp.dot(head_queries, head_keys.T, preferred_element_type=jnp.float32) * scale_factor
        scores = jnp.where(key_live[None, :], scores, -jnp.inf)
        peak = lax.optimization_barrier(jnp.max(scores, axis=1, keepdims=True))
        weights = jnp.exp(scores - peak)
        totals = lax.optimization_barrier(jnp.sum(weights, axis=1, keepdims=True))
        blended = jnp.dot(weights.astype(jnp.bfloat16), head_values, preferred_element_type=jnp.float32)
        return (blended / totals).astype(jnp.bfloat16)
    attended = lax.map(one_head, (queries.transpose(1, 0, 2), keys_all.transpose(1, 0, 2), values_all.transpose(1, 0, 2)))
    attended = attended.transpose(1, 0, 2).reshape(TILES * PIX, HEADS * HEAD)
    projected = jnp.dot(attended, out_weight, preferred_element_type=jnp.float32)
    state = hidden.reshape(TILES * PIX, D).astype(jnp.float32) + gate * (projected + mlp_term.reshape(TILES * PIX, D).astype(jnp.float32))
    centered = state - lax.optimization_barrier(jnp.mean(state, axis=-1, keepdims=True))
    normed = centered * lax.rsqrt(lax.optimization_barrier(jnp.mean(centered * centered, axis=-1, keepdims=True)) + 1e-06)
    modulated = (normed * (1.0 + final_scale) + final_shift).astype(jnp.bfloat16)
    velocity = jnp.dot(modulated, final_weight, preferred_element_type=jnp.float32) + final_bias
    velocity = jnp.where(patch_live[:, None], velocity, 0.0)
    latent_next = latent.reshape(TILES * PIX, LAT) + euler_step(image_size, timestep) * velocity
    return (velocity.reshape(TILES, PIX, LAT), latent_next.reshape(TILES, PIX, LAT))
```

```python
import math

import jax
import jax.numpy as jnp
import numpy as np
from jax import lax
from jax.experimental import pallas as pl
from jax.experimental.pallas import tpu as pltpu
from jax.sharding import PartitionSpec as P

HEAD = 128
STEPS = 28
CANVAS = 48
TILES = 16
GRID_X = 4
TILE_H = 12
TILE_W = 12
PIX = TILE_H * TILE_W
SLOTS = 32
KEYS = PIX + SLOTS
GROUP = 8
HALF_KEYS = GROUP * KEYS
DEAD = -1e30
EXP_SCALE = HEAD ** (-0.5) * math.log2(math.e)
VMEM_LIMIT = 48 * 1024 * 1024


def position_tables():
    tile = np.arange(TILES)[:, None]
    local = np.arange(PIX)[None, :]
    row = tile // GRID_X * TILE_H + local // TILE_W
    col = tile % GRID_X * TILE_W + local % TILE_W
    return row, col


def rope_tables():
    row, col = position_tables()
    side_dims = (HEAD - HEAD // 8) // 2
    side_index = np.arange(side_dims // 2, dtype=np.float32)
    frequency = np.power(np.float32(10000.0), np.float32(-2.0) * side_index / np.float32(side_dims)).astype(np.float32)
    still = np.zeros(row.shape + (HEAD // 16,), np.float32)
    angles = np.concatenate(
        [
            still,
            row[..., None].astype(np.float32) * frequency,
            col[..., None].astype(np.float32) * frequency,
        ],
        axis=-1,
    ).astype(np.float64)
    cosine = np.repeat(np.cos(angles), 2, axis=-1)
    sine = np.repeat(np.sin(angles), 2, axis=-1)
    sine[..., 0::2] *= -1.0
    return cosine.astype(np.float32), sine.astype(np.float32)


def key_tables():
    row, col = position_tables()
    row = row[:GROUP]
    col = col[:GROUP]
    far = np.full((GROUP, SLOTS), 1 << 20)
    slot = np.arange(GROUP * SLOTS).reshape(GROUP, SLOTS)
    key_row = np.concatenate([row, far], axis=1).reshape(1, HALF_KEYS)
    key_col = np.concatenate([col, far], axis=1).reshape(1, HALF_KEYS)
    key_slot = np.concatenate([np.full((GROUP, PIX), 1 << 20), slot], axis=1).reshape(1, HALF_KEYS)
    return np.concatenate([key_row, key_col, key_slot], axis=0).astype(np.int32)


def value_kernel(image_ref, text_ref, out_ref):
    for head in range(GROUP):
        lanes = slice(head * HEAD, (head + 1) * HEAD)
        out_ref[head, 0:PIX, :] = image_ref[0, :, lanes]
        out_ref[head, PIX:KEYS, :] = text_ref[0, :, lanes]


def normed(vectors, gain):
    wide = vectors.astype(jnp.float32)
    return wide * lax.rsqrt(jnp.mean(wide * wide, axis=-1, keepdims=True) + 1e-06) * gain


def query_key_kernel(tile_ref, query_ref, key_ref, text_ref, q_gain_ref, k_gain_ref, cos_ref, sin_ref, out_ref):
    cosine = cos_ref[0]
    sine = sin_ref[0]
    even = lax.broadcasted_iota(jnp.int32, (PIX, HEAD), 1) % 2 == 0

    def rotated(vectors, gain):
        scaled = normed(vectors, gain)
        swapped = jnp.where(even, pltpu.roll(scaled, HEAD - 1, 1), pltpu.roll(scaled, 1, 1))
        return (scaled * cosine + swapped * sine).astype(jnp.bfloat16)

    for head in range(GROUP):
        lanes = slice(head * HEAD, (head + 1) * HEAD)
        out_ref[head, 0:PIX, :] = rotated(query_ref[0, :, lanes], q_gain_ref[...])
        out_ref[head, PIX : 2 * PIX, :] = rotated(key_ref[0, :, lanes], k_gain_ref[...])
        out_ref[head, 2 * PIX :, :] = normed(text_ref[0, :, lanes], k_gain_ref[...]).astype(jnp.bfloat16)


def key_bias(table_ref, size_ref, text_len_ref, half):
    rows = size_ref[0] - half * (CANVAS // 2)
    slots = text_len_ref[0] - half * (GROUP * SLOTS)
    image_ok = (table_ref[0:1, :] < rows) & (table_ref[1:2, :] < size_ref[1])
    text_ok = table_ref[2:3, :] < slots
    return jnp.where(image_ok | text_ok, 0.0, DEAD)


def scores_of(queries, keys, bias):
    scores = lax.dot_general(queries, keys, (((1,), (1,)), ((), ())), preferred_element_type=jnp.float32)
    return scores + bias


def local_kernel(half_ref, size_ref, text_len_ref, table_ref, qk_ref, values_ref, acc_ref, peak_ref, key_s, value_s):
    bias = key_bias(table_ref, size_ref, text_len_ref, half_ref[0])
    for tile in range(GROUP):
        key_s[tile * KEYS : (tile + 1) * KEYS, :] = qk_ref[tile, PIX:, :]
        value_s[tile * KEYS : (tile + 1) * KEYS, 0:HEAD] = values_ref[tile, 0:KEYS, :]
    value_s[:, HEAD:] = jnp.ones((HALF_KEYS, HEAD), jnp.bfloat16)
    for tile in range(GROUP):
        scores = scores_of(qk_ref[tile, 0:PIX, :], key_s[...], bias)
        peak = jnp.max(scores, axis=1, keepdims=True)
        weights = jnp.exp2((scores - peak) * EXP_SCALE).astype(jnp.bfloat16)
        acc_ref[tile] = jnp.dot(weights, value_s[...], preferred_element_type=jnp.float32)
        peak_ref[tile] = jnp.broadcast_to(peak, (PIX, HEAD))


def remote_kernel(
    half_ref, size_ref, text_len_ref, table_ref, qk_ref, keys_ref, values_ref, acc_ref, peak_ref, out_ref, key_s, value_s
):
    bias = key_bias(table_ref, size_ref, text_len_ref, 1 - half_ref[0])
    for tile in range(GROUP):
        key_s[tile * KEYS : (tile + 1) * KEYS, :] = keys_ref[tile]
        value_s[tile * KEYS : (tile + 1) * KEYS, 0:HEAD] = values_ref[tile, KEYS:, :]
    value_s[:, HEAD:] = jnp.ones((HALF_KEYS, HEAD), jnp.bfloat16)
    for tile in range(GROUP):
        scores = scores_of(qk_ref[tile, 0:PIX, :], key_s[...], bias)
        before = peak_ref[tile]
        peak = jnp.maximum(before[:, 0:1], jnp.max(scores, axis=1, keepdims=True))
        weights = jnp.exp2((scores - peak) * EXP_SCALE).astype(jnp.bfloat16)
        factor = jnp.exp2((before - peak) * EXP_SCALE)
        added = jnp.dot(weights, value_s[...], preferred_element_type=jnp.float32)
        blended = acc_ref[tile, :, 0:HEAD] * factor + added[:, 0:HEAD]
        total = acc_ref[tile, :, HEAD:] * factor + added[:, HEAD:]
        out_ref[tile] = (blended / total).astype(jnp.bfloat16)


def project_kernel(attended_ref, weight_ref, out_ref):
    attended = jnp.concatenate([attended_ref[head] for head in range(GROUP)], axis=1)
    out_ref[...] = jnp.dot(attended, weight_ref[...], preferred_element_type=jnp.float32).astype(jnp.bfloat16)


def final_kernel(
    tile_ref,
    size_ref,
    timestep_ref,
    local_ref,
    own_ref,
    other_ref,
    hidden_ref,
    mlp_ref,
    gate_ref,
    shift_ref,
    scale_ref,
    weight_ref,
    bias_ref,
    latent_ref,
    velocity_ref,
    next_ref,
    modulated_s,
):
    rows = 16
    for start in range(0, PIX, rows):
        block = slice(start, start + rows)
        projected = own_ref[block, :].astype(jnp.float32) + other_ref[block, :].astype(jnp.float32)
        state = hidden_ref[block, :].astype(jnp.float32) + gate_ref[...] * (
            projected + mlp_ref[block, :].astype(jnp.float32)
        )
        centered = state - jnp.mean(state, axis=-1, keepdims=True)
        scaled = centered * lax.rsqrt(jnp.mean(centered * centered, axis=-1, keepdims=True) + 1e-06)
        modulated_s[block, :] = (scaled * (1.0 + scale_ref[...]) + shift_ref[...]).astype(jnp.bfloat16)
    latents = weight_ref.shape[0]
    diagonal = lax.broadcasted_iota(jnp.int32, (latents, latents), 0) == lax.broadcasted_iota(
        jnp.int32, (latents, latents), 1
    )
    bias = jnp.sum(jnp.where(diagonal, bias_ref[...], 0.0), axis=1, keepdims=True)
    velocity = (
        lax.dot_general(
            weight_ref[...], modulated_s[...], (((1,), (1,)), ((), ())), preferred_element_type=jnp.float32
        )
        + bias
    )
    tile = tile_ref[0]
    tile_row = tile // GRID_X
    tile_col = tile - tile_row * GRID_X
    live = (local_ref[0:1, :] < size_ref[0] - tile_row * TILE_H) & (local_ref[1:2, :] < size_ref[1] - tile_col * TILE_W)
    velocity = jnp.where(live, velocity, 0.0)
    area = jnp.full((1, PIX), size_ref[0] * size_ref[1], jnp.int32).astype(jnp.float32)
    moment = jnp.full((1, PIX), timestep_ref[0], jnp.int32).astype(jnp.float32)
    shift_factor = jnp.exp(0.5 + 0.65 * (area - 256.0) / 3840.0)
    now_time = 1.0 - moment / STEPS
    next_time = 1.0 - (moment + 1.0) / STEPS

    def sigma_of(at):
        return shift_factor * at / (shift_factor * at + 1.0 - at)

    step = sigma_of(next_time) - sigma_of(now_time)
    velocity_ref[...] = velocity
    next_ref[...] = latent_ref[...] + step * velocity


def whole(shape, index=None):
    at = index if index is not None else (0,) * len(shape)
    return pl.BlockSpec(shape, lambda *_: at)


SMEM = pl.BlockSpec(memory_space=pltpu.SMEM)


def params():
    return pltpu.CompilerParams(vmem_limit_bytes=VMEM_LIMIT)


def shards(
    image_qkv,
    text_kv,
    q_gain,
    k_gain,
    out_weight,
    hidden,
    mlp_term,
    gate,
    final_shift,
    final_scale,
    final_weight,
    final_bias,
    latent,
    image_size,
    text_len,
    timestep,
):
    bf16 = jnp.bfloat16
    width = GROUP * HEAD
    model = hidden.shape[2]
    latents = final_weight.shape[1]
    tile = lax.axis_index("tile").astype(jnp.int32).reshape(1)
    half = tile // GROUP
    triple = image_qkv.reshape(PIX, 3, width).transpose(1, 0, 2)
    text = text_kv.transpose(1, 0, 2)
    groups = [list(range(GROUP)), list(range(GROUP, 2 * GROUP))]
    across = [(t, (t + GROUP) % TILES) for t in range(TILES)]

    values = pl.pallas_call(
        value_kernel,
        grid=(1,),
        in_specs=[whole((1, PIX, width), (2, 0, 0)), whole((1, SLOTS, width), (1, 0, 0))],
        out_specs=whole((GROUP, KEYS, HEAD)),
        out_shape=jax.ShapeDtypeStruct((GROUP, KEYS, HEAD), bf16),
        name="value_layout",
    )(triple, text)
    far_values = lax.ppermute(values, "tile", across)

    cosine, sine = rope_tables()
    spot = pl.BlockSpec((1, PIX, HEAD), lambda i, tile_ref: (tile_ref[0], 0, 0))
    query_key = pl.pallas_call(
        query_key_kernel,
        grid_spec=pltpu.PrefetchScalarGridSpec(
            num_scalar_prefetch=1,
            grid=(1,),
            in_specs=[
                whole((1, PIX, width), (0, 0, 0)),
                whole((1, PIX, width), (1, 0, 0)),
                whole((1, SLOTS, width), (0, 0, 0)),
                whole((1, HEAD)),
                whole((1, HEAD)),
                spot,
                spot,
            ],
            out_specs=whole((GROUP, PIX + KEYS, HEAD)),
        ),
        out_shape=jax.ShapeDtypeStruct((GROUP, PIX + KEYS, HEAD), bf16),
        name="query_key_norm",
    )(tile, triple, triple, text, q_gain.reshape(1, HEAD), k_gain.reshape(1, HEAD), jnp.asarray(cosine), jnp.asarray(sine))
    query_key = lax.all_to_all(query_key, "tile", 0, 0, axis_index_groups=groups, tiled=True)
    far_keys = lax.ppermute(query_key[:, PIX:, :], "tile", across)
    value_pair = lax.all_to_all(
        jnp.concatenate([values, far_values], axis=1), "tile", 0, 0, axis_index_groups=groups, tiled=True
    )

    table = jnp.asarray(key_tables())
    acc, peak = pl.pallas_call(
        local_kernel,
        in_specs=[SMEM, SMEM, SMEM] + [pl.BlockSpec(memory_space=pltpu.VMEM)] * 3,
        out_specs=(pl.BlockSpec(memory_space=pltpu.VMEM),) * 2,
        out_shape=(
            jax.ShapeDtypeStruct((GROUP, PIX, 2 * HEAD), jnp.float32),
            jax.ShapeDtypeStruct((GROUP, PIX, HEAD), jnp.float32),
        ),
        scratch_shapes=[pltpu.VMEM((HALF_KEYS, HEAD), bf16), pltpu.VMEM((HALF_KEYS, 2 * HEAD), bf16)],
        compiler_params=params(),
        name="attend_local",
    )(half, image_size, text_len, table, query_key, value_pair)
    attended = pl.pallas_call(
        remote_kernel,
        in_specs=[SMEM, SMEM, SMEM] + [pl.BlockSpec(memory_space=pltpu.VMEM)] * 6,
        out_specs=pl.BlockSpec(memory_space=pltpu.VMEM),
        out_shape=jax.ShapeDtypeStruct((GROUP, PIX, HEAD), bf16),
        scratch_shapes=[pltpu.VMEM((HALF_KEYS, HEAD), bf16), pltpu.VMEM((HALF_KEYS, 2 * HEAD), bf16)],
        compiler_params=params(),
        name="attend_far",
    )(half, image_size, text_len, table, query_key, far_keys, value_pair, acc, peak)
    attended = lax.all_to_all(attended, "tile", 0, 0, axis_index_groups=groups, tiled=True)

    columns = 768
    own = pl.pallas_call(
        project_kernel,
        grid=(model // columns,),
        in_specs=[whole((GROUP, PIX, HEAD)), pl.BlockSpec((width, columns), lambda i: (0, i))],
        out_specs=pl.BlockSpec((PIX, columns), lambda i: (0, i)),
        out_shape=jax.ShapeDtypeStruct((PIX, model), bf16),
        compiler_params=params(),
        name="project",
    )(attended, out_weight)
    other = lax.ppermute(own, "tp", [(0, 1), (1, 0)])

    local = np.stack([np.arange(PIX) // TILE_W, np.arange(PIX) % TILE_W]).astype(np.int32)
    velocity, latent_next = pl.pallas_call(
        final_kernel,
        in_specs=[SMEM, SMEM, SMEM] + [pl.BlockSpec(memory_space=pltpu.VMEM)] * 11,
        out_specs=(pl.BlockSpec(memory_space=pltpu.VMEM),) * 2,
        out_shape=(jax.ShapeDtypeStruct((latents, PIX), jnp.float32),) * 2,
        scratch_shapes=[pltpu.VMEM((PIX, model), bf16)],
        compiler_params=params(),
        name="final_layer",
    )(
        tile,
        image_size,
        timestep,
        jnp.asarray(local),
        own,
        other,
        hidden.reshape(PIX, model),
        mlp_term.reshape(PIX, model),
        gate.reshape(1, model),
        final_shift.reshape(1, model),
        final_scale.reshape(1, model),
        final_weight.T,
        final_bias.reshape(1, latents),
        latent.reshape(PIX, latents).T,
    )
    return (velocity.T.reshape(1, PIX, latents), latent_next.T.reshape(1, PIX, latents))


def solution(mesh):
    placed = (
        P(("req", "tile"), None, None, "tp"),
        P(("req", "tile"), None, "tp"),
        P(),
        P(),
        P("tp", None),
        P(("req", "tile"), None, None),
        P(("req", "tile"), None, None),
        P("req"),
        P("req"),
        P("req"),
        P(),
        P(),
        P(("req", "tile"), None, None),
        P("req"),
        P("req"),
        P("req"),
    )
    return jax.shard_map(
        shards,
        mesh=mesh,
        in_specs=placed,
        out_specs=(P(("req", "tile"), None, None), P(("req", "tile"), None, None)),
        check_vma=False,
    )
```

```python
import math

import jax
import jax.numpy as jnp
import numpy as np
from jax import lax
from jax.experimental import pallas as pl
from jax.experimental.pallas import tpu as pltpu
from jax.sharding import PartitionSpec as P

HEAD = 128
STEPS = 28
CANVAS = 48
TILES = 16
GRID_X = 4
TILE_H = 12
TILE_W = 12
PIX = TILE_H * TILE_W
SLOTS = 32
KEYS = PIX + SLOTS
GROUP = 8
HALF_KEYS = GROUP * KEYS
DEAD = -1e30
EXP_SCALE = HEAD ** (-0.5) * math.log2(math.e)


def position_tables():
    tile = np.arange(TILES)[:, None]
    local = np.arange(PIX)[None, :]
    row = tile // GRID_X * TILE_H + local // TILE_W
    col = tile % GRID_X * TILE_W + local % TILE_W
    return row, col


def rope_tables():
    row, col = position_tables()
    side_dims = (HEAD - HEAD // 8) // 2
    side_index = np.arange(side_dims // 2, dtype=np.float32)
    frequency = np.power(np.float32(10000.0), np.float32(-2.0) * side_index / np.float32(side_dims)).astype(np.float32)
    still = np.zeros(row.shape + (HEAD // 16,), np.float32)
    angles = np.concatenate(
        [
            still,
            row[..., None].astype(np.float32) * frequency,
            col[..., None].astype(np.float32) * frequency,
        ],
        axis=-1,
    ).astype(np.float64)
    cosine = np.repeat(np.cos(angles), 2, axis=-1)
    sine = np.repeat(np.sin(angles), 2, axis=-1)
    sine[..., 0::2] *= -1.0
    return np.stack([cosine, sine], axis=1).astype(np.float32)


def key_tables():
    row, col = position_tables()
    row = row[:GROUP]
    col = col[:GROUP]
    far = np.full((GROUP, SLOTS), 1 << 20)
    slot = np.arange(GROUP * SLOTS).reshape(GROUP, SLOTS)
    key_row = np.concatenate([row, far], axis=1).reshape(1, HALF_KEYS)
    key_col = np.concatenate([col, far], axis=1).reshape(1, HALF_KEYS)
    key_slot = np.concatenate([np.full((GROUP, PIX), 1 << 20), slot], axis=1).reshape(1, HALF_KEYS)
    return np.concatenate([key_row, key_col, key_slot], axis=0).astype(np.int32)


def normed(vectors, gain):
    wide = vectors.astype(jnp.float32)
    return wide * lax.rsqrt(jnp.mean(wide * wide, axis=-1, keepdims=True) + 1e-06) * gain


def prepare_kernel(
    tile_ref, image_ref, text_ref, q_gain_ref, k_gain_ref, table_ref, out_ref, value_ref
):
    cosine = table_ref[0, 0]
    sine = table_ref[0, 1]
    even = lax.broadcasted_iota(jnp.int32, (PIX, HEAD), 1) % 2 == 0

    def rotated(vectors, gain):
        scaled = normed(vectors, gain)
        swapped = jnp.where(even, pltpu.roll(scaled, HEAD - 1, 1), pltpu.roll(scaled, 1, 1))
        return (scaled * cosine + swapped * sine).astype(jnp.bfloat16)

    text = text_ref[...]
    text_keys = text[:, 0, :]
    text_values = text[:, 1, :]
    for head in range(out_ref.shape[0]):
        lanes = slice(head * HEAD, (head + 1) * HEAD)
        out_ref[head, 0:PIX, :] = rotated(image_ref[0, :, lanes], q_gain_ref[...])
        out_ref[head, PIX : 2 * PIX, :] = rotated(image_ref[1, :, lanes], k_gain_ref[...])
        out_ref[head, 2 * PIX : PIX + KEYS, :] = normed(text_keys[:, lanes], k_gain_ref[...]).astype(jnp.bfloat16)
        for ref, start in ((out_ref, PIX + KEYS), (value_ref, 0)):
            ref[head, start : start + PIX, :] = image_ref[2, :, lanes]
            ref[head, start + PIX : start + KEYS, :] = text_values[:, lanes]


def key_bias(table_ref, size_ref, text_len_ref, half):
    rows = size_ref[0] - half * (CANVAS // 2)
    slots = text_len_ref[0] - half * (GROUP * SLOTS)
    image_ok = (table_ref[0:1, :] < rows) & (table_ref[1:2, :] < size_ref[1])
    text_ok = table_ref[2:3, :] < slots
    return jnp.where(image_ok | text_ok, 0.0, DEAD)


def scores_of(queries, keys, bias):
    scores = lax.dot_general(queries, keys, (((1,), (1,)), ((), ())), preferred_element_type=jnp.float32)
    return scores + bias


def stage(keys_ref, key_start, values_ref, value_start, key_s, value_s):
    for tile in range(GROUP):
        at = tile * KEYS
        key_s[at : at + KEYS, :] = keys_ref[tile, key_start : key_start + KEYS, :]
        value_s[at : at + KEYS, 0:HEAD] = values_ref[tile, value_start : value_start + KEYS, :]
    value_s[:, HEAD:] = jnp.ones((HALF_KEYS, HEAD), jnp.bfloat16)


def local_kernel(half_ref, size_ref, text_len_ref, table_ref, own_ref, acc_ref, peak_ref, key_s, value_s):
    bias = key_bias(table_ref, size_ref, text_len_ref, half_ref[0])
    stage(own_ref, PIX, own_ref, PIX + KEYS, key_s, value_s)
    for tile in range(GROUP):
        scores = scores_of(own_ref[tile, 0:PIX, :], key_s[...], bias)
        peak = jnp.max(scores, axis=1, keepdims=True)
        weights = jnp.exp2((scores - peak) * EXP_SCALE).astype(jnp.bfloat16)
        acc_ref[tile] = jnp.dot(weights, value_s[...], preferred_element_type=jnp.float32)
        peak_ref[tile] = jnp.broadcast_to(peak, (PIX, HEAD))


def remote_kernel(
    half_ref, size_ref, text_len_ref, table_ref, own_ref, keys_ref, values_ref, acc_ref, peak_ref, out_ref, key_s, value_s
):
    bias = key_bias(table_ref, size_ref, text_len_ref, 1 - half_ref[0])
    stage(keys_ref, 0, values_ref, 0, key_s, value_s)
    for tile in range(GROUP):
        scores = scores_of(own_ref[tile, 0:PIX, :], key_s[...], bias)
        before = peak_ref[tile]
        peak = jnp.maximum(before[:, 0:1], jnp.max(scores, axis=1, keepdims=True))
        weights = jnp.exp2((scores - peak) * EXP_SCALE).astype(jnp.bfloat16)
        factor = jnp.exp2((before - peak) * EXP_SCALE)
        added = jnp.dot(weights, value_s[...], preferred_element_type=jnp.float32)
        blended = acc_ref[tile, :, 0:HEAD] * factor + added[:, 0:HEAD]
        total = acc_ref[tile, :, HEAD:] * factor + added[:, HEAD:]
        out_ref[tile] = (blended / total).astype(jnp.bfloat16)


def project_kernel(attended_ref, weight_ref, out_ref):
    attended = jnp.concatenate([attended_ref[head] for head in range(GROUP)], axis=1)
    out_ref[...] = jnp.dot(attended, weight_ref[...], preferred_element_type=jnp.float32).astype(jnp.bfloat16)


def final_kernel(
    tile_ref,
    size_ref,
    timestep_ref,
    local_ref,
    own_ref,
    other_ref,
    hidden_ref,
    mlp_ref,
    gate_ref,
    shift_ref,
    scale_ref,
    weight_ref,
    bias_ref,
    latent_ref,
    velocity_ref,
    next_ref,
    modulated_s,
):
    rows = 16
    for start in range(0, PIX, rows):
        block = slice(start, start + rows)
        projected = own_ref[block, :].astype(jnp.float32) + other_ref[block, :].astype(jnp.float32)
        state = hidden_ref[block, :].astype(jnp.float32) + gate_ref[...] * (
            projected + mlp_ref[block, :].astype(jnp.float32)
        )
        centered = state - jnp.mean(state, axis=-1, keepdims=True)
        scaled = centered * lax.rsqrt(jnp.mean(centered * centered, axis=-1, keepdims=True) + 1e-06)
        modulated_s[block, :] = (scaled * (1.0 + scale_ref[...]) + shift_ref[...]).astype(jnp.bfloat16)
    latents = weight_ref.shape[0]
    diagonal = lax.broadcasted_iota(jnp.int32, (latents, latents), 0) == lax.broadcasted_iota(
        jnp.int32, (latents, latents), 1
    )
    bias = jnp.sum(jnp.where(diagonal, bias_ref[...], 0.0), axis=1, keepdims=True)
    velocity = (
        lax.dot_general(
            weight_ref[...], modulated_s[...], (((1,), (1,)), ((), ())), preferred_element_type=jnp.float32
        )
        + bias
    )
    tile = tile_ref[0]
    tile_row = tile // GRID_X
    tile_col = tile - tile_row * GRID_X
    live = (local_ref[0:1, :] < size_ref[0] - tile_row * TILE_H) & (local_ref[1:2, :] < size_ref[1] - tile_col * TILE_W)
    velocity = jnp.where(live, velocity, 0.0)
    area = jnp.full((1, PIX), size_ref[0] * size_ref[1], jnp.int32).astype(jnp.float32)
    moment = jnp.full((1, PIX), timestep_ref[0], jnp.int32).astype(jnp.float32)
    shift_factor = jnp.exp(0.5 + 0.65 * (area - 256.0) / 3840.0)
    now_time = 1.0 - moment / STEPS
    next_time = 1.0 - (moment + 1.0) / STEPS

    def sigma_of(at):
        return shift_factor * at / (shift_factor * at + 1.0 - at)

    step = sigma_of(next_time) - sigma_of(now_time)
    velocity_ref[...] = velocity
    next_ref[...] = latent_ref[...] + step * velocity


SMEM = pl.BlockSpec(memory_space=pltpu.SMEM)
VMEM = pl.BlockSpec(memory_space=pltpu.VMEM)
HBM = pl.BlockSpec(memory_space=pltpu.HBM)


def params(mebibytes):
    return pltpu.CompilerParams(vmem_limit_bytes=mebibytes * 1024 * 1024)


def shards(
    image_qkv,
    text_kv,
    q_gain,
    k_gain,
    out_weight,
    hidden,
    mlp_term,
    gate,
    final_shift,
    final_scale,
    final_weight,
    final_bias,
    latent,
    image_size,
    text_len,
    timestep,
):
    bf16 = jnp.bfloat16
    width = GROUP * HEAD
    model = hidden.shape[2]
    latents = final_weight.shape[1]
    tile = lax.axis_index("tile").astype(jnp.int32).reshape(1)
    half = tile // GROUP
    triple = image_qkv.reshape(PIX, 3, width).transpose(1, 0, 2)
    groups = [list(range(GROUP)), list(range(GROUP, 2 * GROUP))]
    across = [(t, (t + GROUP) % TILES) for t in range(TILES)]

    per_step = 2
    prepared, values = pl.pallas_call(
        prepare_kernel,
        grid_spec=pltpu.PrefetchScalarGridSpec(
            num_scalar_prefetch=1,
            grid=(GROUP // per_step,),
            in_specs=[
                pl.BlockSpec((3, PIX, per_step * HEAD), lambda i, tile_ref: (0, 0, i)),
                pl.BlockSpec((SLOTS, 2, per_step * HEAD), lambda i, tile_ref: (0, 0, i)),
                pl.BlockSpec((1, HEAD), lambda i, tile_ref: (0, 0)),
                pl.BlockSpec((1, HEAD), lambda i, tile_ref: (0, 0)),
                pl.BlockSpec((1, 2, PIX, HEAD), lambda i, tile_ref: (tile_ref[0], 0, 0, 0)),
            ],
            out_specs=(
                pl.BlockSpec((per_step, PIX + 2 * KEYS, HEAD), lambda i, tile_ref: (i, 0, 0)),
                pl.BlockSpec((per_step, KEYS, HEAD), lambda i, tile_ref: (i, 0, 0)),
            ),
        ),
        out_shape=(
            jax.ShapeDtypeStruct((GROUP, PIX + 2 * KEYS, HEAD), bf16),
            jax.ShapeDtypeStruct((GROUP, KEYS, HEAD), bf16),
        ),
        compiler_params=params(8),
        name="prepare",
    )(tile, triple, text_kv, q_gain.reshape(1, HEAD), k_gain.reshape(1, HEAD), jnp.asarray(rope_tables()))
    far_values = lax.ppermute(values, "tile", across)
    own = lax.all_to_all(prepared, "tile", 0, 0, axis_index_groups=groups, tiled=True)
    far_keys = lax.ppermute(own[:, PIX : PIX + KEYS, :], "tile", across)
    far_values = lax.all_to_all(far_values, "tile", 0, 0, axis_index_groups=groups, tiled=True)

    table = jnp.asarray(key_tables())
    acc, peak = pl.pallas_call(
        local_kernel,
        in_specs=[SMEM, SMEM, SMEM] + [VMEM] * 2,
        out_specs=(VMEM, VMEM),
        out_shape=(
            jax.ShapeDtypeStruct((GROUP, PIX, 2 * HEAD), jnp.float32),
            jax.ShapeDtypeStruct((GROUP, PIX, HEAD), jnp.float32),
        ),
        scratch_shapes=[pltpu.VMEM((HALF_KEYS, HEAD), bf16), pltpu.VMEM((HALF_KEYS, 2 * HEAD), bf16)],
        compiler_params=params(16),
        name="attend_local",
    )(half, image_size, text_len, table, own)
    attended = pl.pallas_call(
        remote_kernel,
        in_specs=[SMEM, SMEM, SMEM] + [VMEM] * 6,
        out_specs=VMEM,
        out_shape=jax.ShapeDtypeStruct((GROUP, PIX, HEAD), bf16),
        scratch_shapes=[pltpu.VMEM((HALF_KEYS, HEAD), bf16), pltpu.VMEM((HALF_KEYS, 2 * HEAD), bf16)],
        compiler_params=params(16),
        name="attend_far",
    )(half, image_size, text_len, table, own, far_keys, far_values, acc, peak)
    attended = lax.all_to_all(attended, "tile", 0, 0, axis_index_groups=groups, tiled=True)

    partial = pl.pallas_call(
        project_kernel,
        in_specs=[VMEM, VMEM],
        out_specs=VMEM,
        out_shape=jax.ShapeDtypeStruct((PIX, model), bf16),
        compiler_params=params(16),
        name="project",
    )(attended, out_weight)
    other = lax.ppermute(partial, "tp", [(0, 1), (1, 0)])

    local = np.stack([np.arange(PIX) // TILE_W, np.arange(PIX) % TILE_W]).astype(np.int32)
    velocity, latent_next = pl.pallas_call(
        final_kernel,
        in_specs=[SMEM, SMEM, SMEM] + [VMEM] * 11,
        out_specs=(VMEM, VMEM),
        out_shape=(jax.ShapeDtypeStruct((latents, PIX), jnp.float32),) * 2,
        scratch_shapes=[pltpu.VMEM((PIX, model), bf16)],
        compiler_params=params(12),
        name="final_layer",
    )(
        tile,
        image_size,
        timestep,
        jnp.asarray(local),
        partial,
        other,
        hidden.reshape(PIX, model),
        mlp_term.reshape(PIX, model),
        gate.reshape(1, model),
        final_shift.reshape(1, model),
        final_scale.reshape(1, model),
        final_weight.T,
        final_bias.reshape(1, latents),
        latent.reshape(PIX, latents).T,
    )
    return (velocity.T.reshape(1, PIX, latents), latent_next.T.reshape(1, PIX, latents))


def solution(mesh):
    placed = (
        P(("req", "tile"), None, None, "tp"),
        P(("req", "tile"), None, "tp"),
        P(),
        P(),
        P("tp", None),
        P(("req", "tile"), None, None),
        P(("req", "tile"), None, None),
        P("req"),
        P("req"),
        P("req"),
        P(),
        P(),
        P(("req", "tile"), None, None),
        P("req"),
        P("req"),
        P("req"),
    )
    return jax.shard_map(
        shards,
        mesh=mesh,
        in_specs=placed,
        out_specs=(P(("req", "tile"), None, None), P(("req", "tile"), None, None)),
        check_vma=False,
    )
```

```python
import math

import jax
import jax.numpy as jnp
import numpy as np
from jax import lax
from jax.experimental import pallas as pl
from jax.experimental.pallas import tpu as pltpu
from jax.sharding import PartitionSpec as P

HEAD = 128
STEPS = 28
CANVAS = 48
TILES = 16
GRID_X = 4
TILE_H = 12
TILE_W = 12
PIX = TILE_H * TILE_W
SLOTS = 32
KEYS = PIX + SLOTS
EARLY = 128
LATE = PIX - EARLY
SENT = KEYS + SLOTS + LATE
GROUP = 8
HALF_KEYS = GROUP * KEYS
DEAD = -1e30
EXP_SCALE = HEAD ** (-0.5) * math.log2(math.e)


def position_tables():
    tile = np.arange(TILES)[:, None]
    local = np.arange(PIX)[None, :]
    row = tile // GRID_X * TILE_H + local // TILE_W
    col = tile % GRID_X * TILE_W + local % TILE_W
    return row, col


def rope_tables():
    row, col = position_tables()
    side_dims = (HEAD - HEAD // 8) // 2
    side_index = np.arange(side_dims // 2, dtype=np.float32)
    frequency = np.power(np.float32(10000.0), np.float32(-2.0) * side_index / np.float32(side_dims)).astype(np.float32)
    still = np.zeros(row.shape + (HEAD // 16,), np.float32)
    angles = np.concatenate(
        [
            still,
            row[..., None].astype(np.float32) * frequency,
            col[..., None].astype(np.float32) * frequency,
        ],
        axis=-1,
    ).astype(np.float64)
    cosine = np.repeat(np.cos(angles), 2, axis=-1)
    sine = np.repeat(np.sin(angles), 2, axis=-1)
    sine[..., 0::2] *= -1.0
    return np.stack([cosine, sine], axis=1).astype(np.float32)


def key_tables():
    row, col = position_tables()
    row = row[:GROUP]
    col = col[:GROUP]
    far = np.full((GROUP, SLOTS), 1 << 20)
    slot = np.arange(GROUP * SLOTS).reshape(GROUP, SLOTS)
    key_row = np.concatenate([row, far], axis=1).reshape(1, HALF_KEYS)
    key_col = np.concatenate([col, far], axis=1).reshape(1, HALF_KEYS)
    key_slot = np.concatenate([np.full((GROUP, PIX), 1 << 20), slot], axis=1).reshape(1, HALF_KEYS)
    return np.concatenate([key_row, key_col, key_slot], axis=0).astype(np.int32)


def normed(vectors, gain):
    wide = vectors.astype(jnp.float32)
    return wide * lax.rsqrt(jnp.mean(wide * wide, axis=-1, keepdims=True) + 1e-06) * gain


def prepare_kernel(
    tile_ref, image_ref, text_ref, q_gain_ref, k_gain_ref, table_ref, out_ref, value_ref
):
    cosine = table_ref[0, 0]
    sine = table_ref[0, 1]
    even = lax.broadcasted_iota(jnp.int32, (PIX, HEAD), 1) % 2 == 0

    def rotated(vectors, gain):
        scaled = normed(vectors, gain)
        swapped = jnp.where(even, pltpu.roll(scaled, HEAD - 1, 1), pltpu.roll(scaled, 1, 1))
        return (scaled * cosine + swapped * sine).astype(jnp.bfloat16)

    text = text_ref[...]
    text_keys = text[:, 0, :]
    text_values = text[:, 1, :]
    for head in range(out_ref.shape[0]):
        lanes = slice(head * HEAD, (head + 1) * HEAD)
        out_ref[head, 0:PIX, :] = rotated(image_ref[0, :, lanes], q_gain_ref[...])
        out_ref[head, PIX : 2 * PIX, :] = rotated(image_ref[1, :, lanes], k_gain_ref[...])
        out_ref[head, 2 * PIX : PIX + KEYS, :] = normed(text_keys[:, lanes], k_gain_ref[...]).astype(jnp.bfloat16)
        out_ref[head, PIX + KEYS : PIX + KEYS + SLOTS, :] = text_values[:, lanes]
        out_ref[head, PIX + KEYS + SLOTS :, :] = image_ref[2, :, lanes]
        value_ref[head] = image_ref[2, LATE:, lanes]


def key_bias(table_ref, size_ref, text_len_ref, half):
    rows = size_ref[0] - half * (CANVAS // 2)
    slots = text_len_ref[0] - half * (GROUP * SLOTS)
    image_ok = (table_ref[0:1, :] < rows) & (table_ref[1:2, :] < size_ref[1])
    text_ok = table_ref[2:3, :] < slots
    return jnp.where(image_ok | text_ok, 0.0, DEAD)


def scores_of(queries, keys, bias):
    scores = lax.dot_general(queries, keys, (((1,), (1,)), ((), ())), preferred_element_type=jnp.float32)
    return scores + bias


def stage(keys_ref, key_start, values_ref, value_start, key_s, value_s):
    text_start = key_start + KEYS
    late_start = text_start + SLOTS
    for tile in range(GROUP):
        at = tile * KEYS
        key_s[at : at + KEYS, :] = keys_ref[tile, key_start:text_start, :]
        value_s[at : at + LATE, 0:HEAD] = keys_ref[tile, late_start : late_start + LATE, :]
        value_s[at + LATE : at + PIX, 0:HEAD] = values_ref[tile, value_start : value_start + EARLY, :]
        value_s[at + PIX : at + KEYS, 0:HEAD] = keys_ref[tile, text_start:late_start, :]
    value_s[:, HEAD:] = jnp.ones((HALF_KEYS, HEAD), jnp.bfloat16)


def local_kernel(half_ref, size_ref, text_len_ref, table_ref, own_ref, acc_ref, peak_ref, key_s, value_s):
    bias = key_bias(table_ref, size_ref, text_len_ref, half_ref[0])
    stage(own_ref, PIX, own_ref, PIX + SENT, key_s, value_s)
    for tile in range(GROUP):
        scores = scores_of(own_ref[tile, 0:PIX, :], key_s[...], bias)
        peak = jnp.max(scores, axis=1, keepdims=True)
        weights = jnp.exp2((scores - peak) * EXP_SCALE).astype(jnp.bfloat16)
        acc_ref[tile] = jnp.dot(weights, value_s[...], preferred_element_type=jnp.float32)
        peak_ref[tile] = jnp.broadcast_to(peak, (PIX, HEAD))


def remote_kernel(
    half_ref, size_ref, text_len_ref, table_ref, own_ref, keys_ref, values_ref, acc_ref, peak_ref, out_ref, key_s, value_s
):
    bias = key_bias(table_ref, size_ref, text_len_ref, 1 - half_ref[0])
    stage(keys_ref, 0, values_ref, 0, key_s, value_s)
    for tile in range(GROUP):
        scores = scores_of(own_ref[tile, 0:PIX, :], key_s[...], bias)
        before = peak_ref[tile]
        peak = jnp.maximum(before[:, 0:1], jnp.max(scores, axis=1, keepdims=True))
        weights = jnp.exp2((scores - peak) * EXP_SCALE).astype(jnp.bfloat16)
        factor = jnp.exp2((before - peak) * EXP_SCALE)
        added = jnp.dot(weights, value_s[...], preferred_element_type=jnp.float32)
        blended = acc_ref[tile, :, 0:HEAD] * factor + added[:, 0:HEAD]
        total = acc_ref[tile, :, HEAD:] * factor + added[:, HEAD:]
        out_ref[tile] = (blended / total).astype(jnp.bfloat16)


def project_kernel(attended_ref, weight_ref, out_ref, weight_s, sems):
    chunks = sems.shape[0]
    columns = weight_s.shape[1] // chunks
    copies = []
    for chunk in range(chunks):
        part = pl.ds(chunk * columns, columns)
        copies.append(pltpu.make_async_copy(weight_ref.at[:, part], weight_s.at[:, part], sems.at[chunk]))
        copies[chunk].start()
    attended = jnp.concatenate([attended_ref[head] for head in range(GROUP)], axis=1)
    for chunk in range(chunks):
        part = slice(chunk * columns, (chunk + 1) * columns)
        copies[chunk].wait()
        out_ref[:, part] = jnp.dot(attended, weight_s[:, part], preferred_element_type=jnp.float32).astype(jnp.bfloat16)


def final_kernel(
    tile_ref,
    size_ref,
    timestep_ref,
    local_ref,
    own_ref,
    other_ref,
    hidden_ref,
    mlp_ref,
    gate_ref,
    shift_ref,
    scale_ref,
    weight_ref,
    bias_ref,
    latent_ref,
    velocity_ref,
    next_ref,
    modulated_s,
):
    rows = 16
    for start in range(0, PIX, rows):
        block = slice(start, start + rows)
        projected = own_ref[block, :].astype(jnp.float32) + other_ref[block, :].astype(jnp.float32)
        state = hidden_ref[block, :].astype(jnp.float32) + gate_ref[...] * (
            projected + mlp_ref[block, :].astype(jnp.float32)
        )
        centered = state - jnp.mean(state, axis=-1, keepdims=True)
        scaled = centered * lax.rsqrt(jnp.mean(centered * centered, axis=-1, keepdims=True) + 1e-06)
        modulated_s[block, :] = (scaled * (1.0 + scale_ref[...]) + shift_ref[...]).astype(jnp.bfloat16)
    latents = weight_ref.shape[0]
    diagonal = lax.broadcasted_iota(jnp.int32, (latents, latents), 0) == lax.broadcasted_iota(
        jnp.int32, (latents, latents), 1
    )
    bias = jnp.sum(jnp.where(diagonal, bias_ref[...], 0.0), axis=1, keepdims=True)
    velocity = (
        lax.dot_general(
            weight_ref[...], modulated_s[...], (((1,), (1,)), ((), ())), preferred_element_type=jnp.float32
        )
        + bias
    )
    tile = tile_ref[0]
    tile_row = tile // GRID_X
    tile_col = tile - tile_row * GRID_X
    live = (local_ref[0:1, :] < size_ref[0] - tile_row * TILE_H) & (local_ref[1:2, :] < size_ref[1] - tile_col * TILE_W)
    velocity = jnp.where(live, velocity, 0.0)
    area = jnp.full((1, PIX), size_ref[0] * size_ref[1], jnp.int32).astype(jnp.float32)
    moment = jnp.full((1, PIX), timestep_ref[0], jnp.int32).astype(jnp.float32)
    shift_factor = jnp.exp(0.5 + 0.65 * (area - 256.0) / 3840.0)
    now_time = 1.0 - moment / STEPS
    next_time = 1.0 - (moment + 1.0) / STEPS

    def sigma_of(at):
        return shift_factor * at / (shift_factor * at + 1.0 - at)

    step = sigma_of(next_time) - sigma_of(now_time)
    velocity_ref[...] = velocity
    next_ref[...] = latent_ref[...] + step * velocity


SMEM = pl.BlockSpec(memory_space=pltpu.SMEM)
VMEM = pl.BlockSpec(memory_space=pltpu.VMEM)
HBM = pl.BlockSpec(memory_space=pltpu.HBM)


def params(mebibytes):
    return pltpu.CompilerParams(vmem_limit_bytes=mebibytes * 1024 * 1024)


def shards(
    image_qkv,
    text_kv,
    q_gain,
    k_gain,
    out_weight,
    hidden,
    mlp_term,
    gate,
    final_shift,
    final_scale,
    final_weight,
    final_bias,
    latent,
    image_size,
    text_len,
    timestep,
):
    bf16 = jnp.bfloat16
    width = GROUP * HEAD
    model = hidden.shape[2]
    latents = final_weight.shape[1]
    tile = lax.axis_index("tile").astype(jnp.int32).reshape(1)
    half = tile // GROUP
    triple = image_qkv.reshape(PIX, 3, width).transpose(1, 0, 2)
    groups = [list(range(GROUP)), list(range(GROUP, 2 * GROUP))]
    across = [(t, (t + GROUP) % TILES) for t in range(TILES)]

    per_step = 2
    prepared, values = pl.pallas_call(
        prepare_kernel,
        grid_spec=pltpu.PrefetchScalarGridSpec(
            num_scalar_prefetch=1,
            grid=(GROUP // per_step,),
            in_specs=[
                pl.BlockSpec((3, PIX, per_step * HEAD), lambda i, tile_ref: (0, 0, i)),
                pl.BlockSpec((SLOTS, 2, per_step * HEAD), lambda i, tile_ref: (0, 0, i)),
                pl.BlockSpec((1, HEAD), lambda i, tile_ref: (0, 0)),
                pl.BlockSpec((1, HEAD), lambda i, tile_ref: (0, 0)),
                pl.BlockSpec((1, 2, PIX, HEAD), lambda i, tile_ref: (tile_ref[0], 0, 0, 0)),
            ],
            out_specs=(
                pl.BlockSpec((per_step, PIX + 2 * KEYS, HEAD), lambda i, tile_ref: (i, 0, 0)),
                pl.BlockSpec((per_step, EARLY, HEAD), lambda i, tile_ref: (i, 0, 0)),
            ),
        ),
        out_shape=(
            jax.ShapeDtypeStruct((GROUP, PIX + 2 * KEYS, HEAD), bf16),
            jax.ShapeDtypeStruct((GROUP, EARLY, HEAD), bf16),
        ),
        name="prepare",
    )(tile, triple, text_kv, q_gain.reshape(1, HEAD), k_gain.reshape(1, HEAD), jnp.asarray(rope_tables()))
    far_values = lax.ppermute(values, "tile", across)
    own = lax.all_to_all(prepared, "tile", 0, 0, axis_index_groups=groups, tiled=True)
    far_keys = lax.ppermute(own[:, PIX : PIX + SENT, :], "tile", across)
    table = jnp.asarray(key_tables())
    acc, peak = pl.pallas_call(
        local_kernel,
        in_specs=[SMEM, SMEM, SMEM] + [VMEM] * 2,
        out_specs=(VMEM, VMEM),
        out_shape=(
            jax.ShapeDtypeStruct((GROUP, PIX, 2 * HEAD), jnp.float32),
            jax.ShapeDtypeStruct((GROUP, PIX, HEAD), jnp.float32),
        ),
        scratch_shapes=[pltpu.VMEM((HALF_KEYS, HEAD), bf16), pltpu.VMEM((HALF_KEYS, 2 * HEAD), bf16)],
        compiler_params=params(16),
        name="attend_local",
    )(half, image_size, text_len, table, own)
    far_values, peak = lax.optimization_barrier((far_values, peak))
    far_values = lax.all_to_all(far_values, "tile", 0, 0, axis_index_groups=groups, tiled=True)
    attended = pl.pallas_call(
        remote_kernel,
        in_specs=[SMEM, SMEM, SMEM] + [VMEM] * 6,
        out_specs=VMEM,
        out_shape=jax.ShapeDtypeStruct((GROUP, PIX, HEAD), bf16),
        scratch_shapes=[pltpu.VMEM((HALF_KEYS, HEAD), bf16), pltpu.VMEM((HALF_KEYS, 2 * HEAD), bf16)],
        compiler_params=params(16),
        name="attend_far",
    )(half, image_size, text_len, table, own, far_keys, far_values, acc, peak)
    attended = lax.all_to_all(attended, "tile", 0, 0, axis_index_groups=groups, tiled=True)

    partial = pl.pallas_call(
        project_kernel,
        in_specs=[VMEM, HBM],
        out_specs=VMEM,
        out_shape=jax.ShapeDtypeStruct((PIX, model), bf16),
        scratch_shapes=[pltpu.VMEM((width, model), bf16), pltpu.SemaphoreType.DMA((6,))],
        compiler_params=params(48),
        name="project",
    )(attended, out_weight)
    other = lax.ppermute(partial, "tp", [(0, 1), (1, 0)])

    local = np.stack([np.arange(PIX) // TILE_W, np.arange(PIX) % TILE_W]).astype(np.int32)
    velocity, latent_next = pl.pallas_call(
        final_kernel,
        in_specs=[SMEM, SMEM, SMEM] + [VMEM] * 11,
        out_specs=(VMEM, VMEM),
        out_shape=(jax.ShapeDtypeStruct((latents, PIX), jnp.float32),) * 2,
        scratch_shapes=[pltpu.VMEM((PIX, model), bf16)],
        compiler_params=params(12),
        name="final_layer",
    )(
        tile,
        image_size,
        timestep,
        jnp.asarray(local),
        partial,
        other,
        hidden.reshape(PIX, model),
        mlp_term.reshape(PIX, model),
        gate.reshape(1, model),
        final_shift.reshape(1, model),
        final_scale.reshape(1, model),
        final_weight.T,
        final_bias.reshape(1, latents),
        latent.reshape(PIX, latents).T,
    )
    return (velocity.T.reshape(1, PIX, latents), latent_next.T.reshape(1, PIX, latents))


def solution(mesh):
    placed = (
        P(("req", "tile"), None, None, "tp"),
        P(("req", "tile"), None, "tp"),
        P(),
        P(),
        P("tp", None),
        P(("req", "tile"), None, None),
        P(("req", "tile"), None, None),
        P("req"),
        P("req"),
        P("req"),
        P(),
        P(),
        P(("req", "tile"), None, None),
        P("req"),
        P("req"),
        P("req"),
    )
    return jax.shard_map(
        shards,
        mesh=mesh,
        in_specs=placed,
        out_specs=(P(("req", "tile"), None, None), P(("req", "tile"), None, None)),
        check_vma=False,
    )
```

```python
import math

import jax
import jax.numpy as jnp
import numpy as np
from jax import lax
from jax.experimental import pallas as pl
from jax.experimental.pallas import tpu as pltpu
from jax.sharding import PartitionSpec as P

HEAD = 128
STEPS = 28
CANVAS = 48
TILES = 16
GRID_X = 4
TILE_H = 12
TILE_W = 12
PIX = TILE_H * TILE_W
SLOTS = 32
KEYS = PIX + SLOTS
GROUP = 8
HALF_KEYS = GROUP * KEYS
DEAD = -1e30
EXP_SCALE = HEAD ** (-0.5) * math.log2(math.e)


def position_tables():
    tile = np.arange(TILES)[:, None]
    local = np.arange(PIX)[None, :]
    row = tile // GRID_X * TILE_H + local // TILE_W
    col = tile % GRID_X * TILE_W + local % TILE_W
    return row, col


def rope_tables():
    row, col = position_tables()
    side_dims = (HEAD - HEAD // 8) // 2
    side_index = np.arange(side_dims // 2, dtype=np.float32)
    frequency = np.power(np.float32(10000.0), np.float32(-2.0) * side_index / np.float32(side_dims)).astype(np.float32)
    still = np.zeros(row.shape + (HEAD // 16,), np.float32)
    angles = np.concatenate(
        [
            still,
            row[..., None].astype(np.float32) * frequency,
            col[..., None].astype(np.float32) * frequency,
        ],
        axis=-1,
    ).astype(np.float64)
    cosine = np.repeat(np.cos(angles), 2, axis=-1)
    sine = np.repeat(np.sin(angles), 2, axis=-1)
    sine[..., 0::2] *= -1.0
    return np.stack([cosine, sine], axis=1).astype(np.float32)


def group_tiles():
    lows = np.arange(TILES // GRID_X)[:, None] * GRID_X
    kinds = [
        [np.arange(GROUP), np.arange(GROUP) + GROUP],
        [(lows + np.array([0, 1])).reshape(-1), (lows + np.array([3, 2])).reshape(-1)],
    ]
    partners = np.zeros((2, TILES), np.int64)
    for kind, (near, far) in enumerate(kinds):
        partners[kind, near] = far
        partners[kind, far] = near
    return kinds, partners


def key_tables():
    row, col = position_tables()
    far = np.full((GROUP, SLOTS), 1 << 20)
    beyond = np.full((GROUP, PIX), 1 << 20)
    tables = []
    for kind in group_tiles()[0]:
        for tiles in kind:
            slot = tiles[:, None] * SLOTS + np.arange(SLOTS)[None, :]
            parts = ((row[tiles], far), (col[tiles], far), (beyond, slot))
            tables.append(np.stack([np.concatenate(part, axis=1).reshape(HALF_KEYS) for part in parts]))
    return np.stack(tables).astype(np.int32)


def normed(vectors, gain):
    wide = vectors.astype(jnp.float32)
    return wide * lax.rsqrt(jnp.mean(wide * wide, axis=-1, keepdims=True) + 1e-06) * gain


def prepare_kernel(
    tile_ref, image_ref, text_ref, q_gain_ref, k_gain_ref, table_ref, out_ref
):
    cosine = table_ref[0, 0]
    sine = table_ref[0, 1]
    even = lax.broadcasted_iota(jnp.int32, (PIX, HEAD), 1) % 2 == 0

    def rotated(vectors, gain):
        scaled = normed(vectors, gain)
        swapped = jnp.where(even, pltpu.roll(scaled, HEAD - 1, 1), pltpu.roll(scaled, 1, 1))
        return (scaled * cosine + swapped * sine).astype(jnp.bfloat16)

    text = text_ref[...]
    text_keys = text[:, 0, :]
    text_values = text[:, 1, :]
    for head in range(out_ref.shape[0]):
        lanes = slice(head * HEAD, (head + 1) * HEAD)
        out_ref[head, 0:PIX, :] = rotated(image_ref[0, :, lanes], q_gain_ref[...])
        out_ref[head, PIX : 2 * PIX, :] = rotated(image_ref[1, :, lanes], k_gain_ref[...])
        out_ref[head, 2 * PIX : PIX + KEYS, :] = normed(text_keys[:, lanes], k_gain_ref[...]).astype(jnp.bfloat16)
        out_ref[head, PIX + KEYS : 2 * PIX + KEYS, :] = image_ref[2, :, lanes]
        out_ref[head, 2 * PIX + KEYS :, :] = text_values[:, lanes]


def key_bias(table_ref, size_ref, text_len_ref, group):
    image_ok = (table_ref[group, 0:1, :] < size_ref[0]) & (table_ref[group, 1:2, :] < size_ref[1])
    text_ok = table_ref[group, 2:3, :] < text_len_ref[0]
    return jnp.where(image_ok | text_ok, 0.0, DEAD)


def scores_of(queries, keys, bias):
    scores = lax.dot_general(queries, keys, (((1,), (1,)), ((), ())), preferred_element_type=jnp.float32)
    return scores + bias


def stage(source_ref, start, key_s, value_s):
    for tile in range(GROUP):
        rows = slice(tile * KEYS, (tile + 1) * KEYS)
        key_s[rows, :] = source_ref[tile, start : start + KEYS, :]
        value_s[rows, 0:HEAD] = source_ref[tile, start + KEYS : start + 2 * KEYS, :]
    value_s[:, HEAD:] = jnp.ones((HALF_KEYS, HEAD), jnp.bfloat16)


def local_kernel(group_ref, size_ref, text_len_ref, table_ref, own_ref, acc_ref, peak_ref, key_s, value_s):
    bias = key_bias(table_ref, size_ref, text_len_ref, group_ref[0])
    stage(own_ref, PIX, key_s, value_s)
    for tile in range(GROUP):
        scores = scores_of(own_ref[tile, 0:PIX, :], key_s[...], bias)
        peak = jnp.max(scores, axis=1, keepdims=True)
        weights = jnp.exp2((scores - peak) * EXP_SCALE).astype(jnp.bfloat16)
        acc_ref[tile] = jnp.dot(weights, value_s[...], preferred_element_type=jnp.float32)
        peak_ref[tile] = jnp.broadcast_to(peak, (PIX, HEAD))


def remote_kernel(
    group_ref, size_ref, text_len_ref, table_ref, own_ref, far_ref, acc_ref, peak_ref, out_ref, key_s, value_s
):
    bias = key_bias(table_ref, size_ref, text_len_ref, group_ref[1])
    stage(far_ref, 0, key_s, value_s)
    for tile in range(GROUP):
        scores = scores_of(own_ref[tile, 0:PIX, :], key_s[...], bias)
        before = peak_ref[tile]
        peak = jnp.maximum(before[:, 0:1], jnp.max(scores, axis=1, keepdims=True))
        weights = jnp.exp2((scores - peak) * EXP_SCALE).astype(jnp.bfloat16)
        factor = jnp.exp2((before - peak) * EXP_SCALE)
        added = jnp.dot(weights, value_s[...], preferred_element_type=jnp.float32)
        blended = acc_ref[tile, :, 0:HEAD] * factor + added[:, 0:HEAD]
        total = acc_ref[tile, :, HEAD:] * factor + added[:, HEAD:]
        out_ref[tile] = (blended / total).astype(jnp.bfloat16)


def project_kernel(attended_ref, weight_ref, out_ref, weight_s, sems):
    chunks = sems.shape[0]
    columns = weight_s.shape[1] // chunks
    copies = []
    for chunk in range(chunks):
        part = pl.ds(chunk * columns, columns)
        copies.append(pltpu.make_async_copy(weight_ref.at[:, part], weight_s.at[:, part], sems.at[chunk]))
        copies[chunk].start()
    attended = jnp.concatenate([attended_ref[head] for head in range(GROUP)], axis=1)
    for chunk in range(chunks):
        part = slice(chunk * columns, (chunk + 1) * columns)
        copies[chunk].wait()
        out_ref[:, part] = jnp.dot(attended, weight_s[:, part], preferred_element_type=jnp.float32).astype(jnp.bfloat16)


def final_kernel(
    tile_ref,
    size_ref,
    timestep_ref,
    local_ref,
    own_ref,
    other_ref,
    hidden_ref,
    mlp_ref,
    gate_ref,
    shift_ref,
    scale_ref,
    weight_ref,
    bias_ref,
    latent_ref,
    velocity_ref,
    next_ref,
    modulated_s,
):
    rows = 16
    for start in range(0, PIX, rows):
        block = slice(start, start + rows)
        projected = own_ref[block, :].astype(jnp.float32) + other_ref[block, :].astype(jnp.float32)
        state = hidden_ref[block, :].astype(jnp.float32) + gate_ref[...] * (
            projected + mlp_ref[block, :].astype(jnp.float32)
        )
        centered = state - jnp.mean(state, axis=-1, keepdims=True)
        scaled = centered * lax.rsqrt(jnp.mean(centered * centered, axis=-1, keepdims=True) + 1e-06)
        modulated_s[block, :] = (scaled * (1.0 + scale_ref[...]) + shift_ref[...]).astype(jnp.bfloat16)
    latents = weight_ref.shape[0]
    diagonal = lax.broadcasted_iota(jnp.int32, (latents, latents), 0) == lax.broadcasted_iota(
        jnp.int32, (latents, latents), 1
    )
    bias = jnp.sum(jnp.where(diagonal, bias_ref[...], 0.0), axis=1, keepdims=True)
    velocity = (
        lax.dot_general(
            weight_ref[...], modulated_s[...], (((1,), (1,)), ((), ())), preferred_element_type=jnp.float32
        )
        + bias
    )
    tile = tile_ref[0]
    tile_row = tile // GRID_X
    tile_col = tile - tile_row * GRID_X
    live = (local_ref[0:1, :] < size_ref[0] - tile_row * TILE_H) & (local_ref[1:2, :] < size_ref[1] - tile_col * TILE_W)
    velocity = jnp.where(live, velocity, 0.0)
    area = jnp.full((1, PIX), size_ref[0] * size_ref[1], jnp.int32).astype(jnp.float32)
    moment = jnp.full((1, PIX), timestep_ref[0], jnp.int32).astype(jnp.float32)
    shift_factor = jnp.exp(0.5 + 0.65 * (area - 256.0) / 3840.0)
    now_time = 1.0 - moment / STEPS
    next_time = 1.0 - (moment + 1.0) / STEPS

    def sigma_of(at):
        return shift_factor * at / (shift_factor * at + 1.0 - at)

    step = sigma_of(next_time) - sigma_of(now_time)
    velocity_ref[...] = velocity
    next_ref[...] = latent_ref[...] + step * velocity


SMEM = pl.BlockSpec(memory_space=pltpu.SMEM)
VMEM = pl.BlockSpec(memory_space=pltpu.VMEM)
HBM = pl.BlockSpec(memory_space=pltpu.HBM)


def params(mebibytes):
    return pltpu.CompilerParams(vmem_limit_bytes=mebibytes * 1024 * 1024)


def shards(
    image_qkv,
    text_kv,
    q_gain,
    k_gain,
    out_weight,
    hidden,
    mlp_term,
    gate,
    final_shift,
    final_scale,
    final_weight,
    final_bias,
    latent,
    image_size,
    text_len,
    timestep,
):
    bf16 = jnp.bfloat16
    width = GROUP * HEAD
    model = hidden.shape[2]
    latents = final_weight.shape[1]
    tile = lax.axis_index("tile").astype(jnp.int32).reshape(1)
    kind = lax.axis_index("tp").astype(jnp.int32)
    which = jnp.where(kind == 0, tile[0] // GROUP, tile[0] % GRID_X // 2)
    group = jnp.stack([2 * kind + which, 2 * kind + 1 - which])
    triple = image_qkv.reshape(PIX, 3, width).transpose(1, 0, 2)
    kinds, partners = group_tiles()
    mesh_axes = ("tile", "tp")
    groups = [[int(t) * 2 + kind for t in tiles] for kind in range(2) for tiles in kinds[kind]]
    across = [(t * 2 + kind, int(partners[kind, t]) * 2 + kind) for t in range(TILES) for kind in range(2)]

    per_step = 2
    prepared = pl.pallas_call(
        prepare_kernel,
        grid_spec=pltpu.PrefetchScalarGridSpec(
            num_scalar_prefetch=1,
            grid=(GROUP // per_step,),
            in_specs=[
                pl.BlockSpec((3, PIX, per_step * HEAD), lambda i, tile_ref: (0, 0, i)),
                pl.BlockSpec((SLOTS, 2, per_step * HEAD), lambda i, tile_ref: (0, 0, i)),
                pl.BlockSpec((1, HEAD), lambda i, tile_ref: (0, 0)),
                pl.BlockSpec((1, HEAD), lambda i, tile_ref: (0, 0)),
                pl.BlockSpec((1, 2, PIX, HEAD), lambda i, tile_ref: (tile_ref[0], 0, 0, 0)),
            ],
            out_specs=pl.BlockSpec((per_step, PIX + 2 * KEYS, HEAD), lambda i, tile_ref: (i, 0, 0)),
        ),
        out_shape=jax.ShapeDtypeStruct((GROUP, PIX + 2 * KEYS, HEAD), bf16),
        name="prepare",
    )(tile, triple, text_kv, q_gain.reshape(1, HEAD), k_gain.reshape(1, HEAD), jnp.asarray(rope_tables()))
    own = lax.all_to_all(prepared, mesh_axes, 0, 0, axis_index_groups=groups, tiled=True)
    far = lax.ppermute(own[:, PIX:, :], mesh_axes, across)

    table = jnp.asarray(key_tables())
    acc, peak = pl.pallas_call(
        local_kernel,
        in_specs=[SMEM, SMEM, SMEM] + [VMEM] * 2,
        out_specs=(VMEM, VMEM),
        out_shape=(
            jax.ShapeDtypeStruct((GROUP, PIX, 2 * HEAD), jnp.float32),
            jax.ShapeDtypeStruct((GROUP, PIX, HEAD), jnp.float32),
        ),
        scratch_shapes=[pltpu.VMEM((HALF_KEYS, HEAD), bf16), pltpu.VMEM((HALF_KEYS, 2 * HEAD), bf16)],
        compiler_params=params(16),
        name="attend_local",
    )(group, image_size, text_len, table, own)
    attended = pl.pallas_call(
        remote_kernel,
        in_specs=[SMEM, SMEM, SMEM] + [VMEM] * 5,
        out_specs=VMEM,
        out_shape=jax.ShapeDtypeStruct((GROUP, PIX, HEAD), bf16),
        scratch_shapes=[pltpu.VMEM((HALF_KEYS, HEAD), bf16), pltpu.VMEM((HALF_KEYS, 2 * HEAD), bf16)],
        compiler_params=params(16),
        name="attend_far",
    )(group, image_size, text_len, table, own, far, acc, peak)
    attended = lax.all_to_all(attended, mesh_axes, 0, 0, axis_index_groups=groups, tiled=True)

    partial = pl.pallas_call(
        project_kernel,
        in_specs=[VMEM, HBM],
        out_specs=VMEM,
        out_shape=jax.ShapeDtypeStruct((PIX, model), bf16),
        scratch_shapes=[pltpu.VMEM((width, model), bf16), pltpu.SemaphoreType.DMA((6,))],
        compiler_params=params(48),
        name="project",
    )(attended, out_weight)
    other = lax.ppermute(partial, "tp", [(0, 1), (1, 0)])

    local = np.stack([np.arange(PIX) // TILE_W, np.arange(PIX) % TILE_W]).astype(np.int32)
    velocity, latent_next = pl.pallas_call(
        final_kernel,
        in_specs=[SMEM, SMEM, SMEM] + [VMEM] * 11,
        out_specs=(VMEM, VMEM),
        out_shape=(jax.ShapeDtypeStruct((latents, PIX), jnp.float32),) * 2,
        scratch_shapes=[pltpu.VMEM((PIX, model), bf16)],
        compiler_params=params(12),
        name="final_layer",
    )(
        tile,
        image_size,
        timestep,
        jnp.asarray(local),
        partial,
        other,
        hidden.reshape(PIX, model),
        mlp_term.reshape(PIX, model),
        gate.reshape(1, model),
        final_shift.reshape(1, model),
        final_scale.reshape(1, model),
        final_weight.T,
        final_bias.reshape(1, latents),
        latent.reshape(PIX, latents).T,
    )
    return (velocity.T.reshape(1, PIX, latents), latent_next.T.reshape(1, PIX, latents))


def solution(mesh):
    placed = (
        P(("req", "tile"), None, None, "tp"),
        P(("req", "tile"), None, "tp"),
        P(),
        P(),
        P("tp", None),
        P(("req", "tile"), None, None),
        P(("req", "tile"), None, None),
        P("req"),
        P("req"),
        P("req"),
        P(),
        P(),
        P(("req", "tile"), None, None),
        P("req"),
        P("req"),
        P("req"),
    )
    return jax.shard_map(
        shards,
        mesh=mesh,
        in_specs=placed,
        out_specs=(P(("req", "tile"), None, None), P(("req", "tile"), None, None)),
        check_vma=False,
    )
```

```python
import math

import jax
import jax.numpy as jnp
import numpy as np
from jax import lax
from jax.experimental import pallas as pl
from jax.experimental.pallas import tpu as pltpu
from jax.sharding import PartitionSpec as P

HEAD = 128
STEPS = 28
CANVAS = 48
TILES = 16
GRID_X = 4
TILE_H = 12
TILE_W = 12
PIX = TILE_H * TILE_W
SLOTS = 32
KEYS = PIX + SLOTS
GROUP = 8
HALF_KEYS = GROUP * KEYS
DEAD = -1e30
EXP_SCALE = HEAD ** (-0.5) * math.log2(math.e)


def position_tables():
    tile = np.arange(TILES)[:, None]
    local = np.arange(PIX)[None, :]
    row = tile // GRID_X * TILE_H + local // TILE_W
    col = tile % GRID_X * TILE_W + local % TILE_W
    return row, col


def rope_tables():
    row, col = position_tables()
    side_dims = (HEAD - HEAD // 8) // 2
    side_index = np.arange(side_dims // 2, dtype=np.float32)
    frequency = np.power(np.float32(10000.0), np.float32(-2.0) * side_index / np.float32(side_dims)).astype(np.float32)
    still = np.zeros(row.shape + (HEAD // 16,), np.float32)
    angles = np.concatenate(
        [
            still,
            row[..., None].astype(np.float32) * frequency,
            col[..., None].astype(np.float32) * frequency,
        ],
        axis=-1,
    ).astype(np.float64)
    cosine = np.repeat(np.cos(angles), 2, axis=-1)
    sine = np.repeat(np.sin(angles), 2, axis=-1)
    sine[..., 0::2] *= -1.0
    return np.stack([cosine, sine], axis=1).astype(np.float32)


def group_tiles():
    lows = np.arange(TILES // GRID_X)[:, None] * GRID_X
    kinds = [
        [np.arange(GROUP), np.arange(GROUP) + GROUP],
        [(lows + np.array([0, 1])).reshape(-1), (lows + np.array([3, 2])).reshape(-1)],
    ]
    partners = np.zeros((2, TILES), np.int64)
    for kind, (near, far) in enumerate(kinds):
        partners[kind, near] = far
        partners[kind, far] = near
    return kinds, partners


def key_tables():
    row, col = position_tables()
    far = np.full((GROUP, SLOTS), 1 << 20)
    beyond = np.full((GROUP, PIX), 1 << 20)
    tables = []
    for kind in group_tiles()[0]:
        for tiles in kind:
            slot = tiles[:, None] * SLOTS + np.arange(SLOTS)[None, :]
            parts = ((row[tiles], far), (col[tiles], far), (beyond, slot))
            tables.append(np.stack([np.concatenate(part, axis=1).reshape(HALF_KEYS) for part in parts]))
    return np.stack(tables).astype(np.int32)


def normed(vectors, gain):
    wide = vectors.astype(jnp.float32)
    return wide * lax.rsqrt(jnp.mean(wide * wide, axis=-1, keepdims=True) + 1e-06) * gain


def rotated(vectors, gain, table_ref):
    scaled = normed(vectors, gain)
    even = lax.broadcasted_iota(jnp.int32, (PIX, HEAD), 1) % 2 == 0
    swapped = jnp.where(even, pltpu.roll(scaled, HEAD - 1, 1), pltpu.roll(scaled, 1, 1))
    return (scaled * table_ref[0, 0] + swapped * table_ref[0, 1]).astype(jnp.bfloat16)


def key_value_kernel(tile_ref, key_ref, value_ref, text_ref, gain_ref, table_ref, out_ref):
    text = text_ref[...]
    text_keys = text[:, 0, :]
    text_values = text[:, 1, :]
    for head in range(out_ref.shape[0]):
        lanes = slice(head * HEAD, (head + 1) * HEAD)
        out_ref[head, 0:PIX, :] = rotated(key_ref[0, :, lanes], gain_ref[...], table_ref)
        out_ref[head, PIX:KEYS, :] = normed(text_keys[:, lanes], gain_ref[...]).astype(jnp.bfloat16)
        out_ref[head, KEYS : KEYS + PIX, :] = value_ref[0, :, lanes]
        out_ref[head, KEYS + PIX :, :] = text_values[:, lanes]


def query_kernel(tile_ref, query_ref, gain_ref, table_ref, out_ref):
    for head in range(out_ref.shape[0]):
        lanes = slice(head * HEAD, (head + 1) * HEAD)
        out_ref[head] = rotated(query_ref[0, :, lanes], gain_ref[...], table_ref)


def key_bias(table_ref, size_ref, text_len_ref, group):
    image_ok = (table_ref[group, 0:1, :] < size_ref[0]) & (table_ref[group, 1:2, :] < size_ref[1])
    text_ok = table_ref[group, 2:3, :] < text_len_ref[0]
    return jnp.where(image_ok | text_ok, 0.0, DEAD)


def scores_of(queries, keys, bias):
    scores = lax.dot_general(queries, keys, (((1,), (1,)), ((), ())), preferred_element_type=jnp.float32)
    return scores + bias


def stage(source_ref, key_s, value_s):
    for tile in range(GROUP):
        rows = slice(tile * KEYS, (tile + 1) * KEYS)
        key_s[rows, :] = source_ref[tile, 0:KEYS, :]
        value_s[rows, 0:HEAD] = source_ref[tile, KEYS:, :]
    value_s[:, HEAD:] = jnp.ones((HALF_KEYS, HEAD), jnp.bfloat16)


def local_kernel(group_ref, size_ref, text_len_ref, table_ref, query_ref, own_ref, acc_ref, peak_ref, key_s, value_s):
    bias = key_bias(table_ref, size_ref, text_len_ref, group_ref[0])
    stage(own_ref, key_s, value_s)
    for tile in range(GROUP):
        scores = scores_of(query_ref[tile], key_s[...], bias)
        peak = jnp.max(scores, axis=1, keepdims=True)
        weights = jnp.exp2((scores - peak) * EXP_SCALE).astype(jnp.bfloat16)
        acc_ref[tile] = jnp.dot(weights, value_s[...], preferred_element_type=jnp.float32)
        peak_ref[tile] = jnp.broadcast_to(peak, (PIX, HEAD))


def remote_kernel(
    group_ref, size_ref, text_len_ref, table_ref, query_ref, far_ref, acc_ref, peak_ref, out_ref, key_s, value_s
):
    bias = key_bias(table_ref, size_ref, text_len_ref, group_ref[1])
    stage(far_ref, key_s, value_s)
    for tile in range(GROUP):
        scores = scores_of(query_ref[tile], key_s[...], bias)
        before = peak_ref[tile]
        peak = jnp.maximum(before[:, 0:1], jnp.max(scores, axis=1, keepdims=True))
        weights = jnp.exp2((scores - peak) * EXP_SCALE).astype(jnp.bfloat16)
        factor = jnp.exp2((before - peak) * EXP_SCALE)
        added = jnp.dot(weights, value_s[...], preferred_element_type=jnp.float32)
        blended = acc_ref[tile, :, 0:HEAD] * factor + added[:, 0:HEAD]
        total = acc_ref[tile, :, HEAD:] * factor + added[:, HEAD:]
        out_ref[tile] = (blended / total).astype(jnp.bfloat16)


def residual_kernel(hidden_ref, mlp_ref, gate_ref, out_ref):
    out_ref[...] = hidden_ref[...].astype(jnp.float32) + gate_ref[...] * mlp_ref[...].astype(jnp.float32)


def project_kernel(attended_ref, weight_ref, out_ref):
    attended = jnp.concatenate([attended_ref[head] for head in range(GROUP)], axis=1)
    out_ref[...] = jnp.dot(attended, weight_ref[...], preferred_element_type=jnp.float32).astype(jnp.bfloat16)


def final_kernel(
    tile_ref,
    size_ref,
    timestep_ref,
    local_ref,
    own_ref,
    other_ref,
    residual_ref,
    gate_ref,
    shift_ref,
    scale_ref,
    weight_ref,
    bias_ref,
    latent_ref,
    velocity_ref,
    next_ref,
    modulated_s,
):
    rows = 16
    for start in range(0, PIX, rows):
        block = slice(start, start + rows)
        projected = own_ref[block, :].astype(jnp.float32) + other_ref[block, :].astype(jnp.float32)
        state = residual_ref[block, :] + gate_ref[...] * projected
        centered = state - jnp.mean(state, axis=-1, keepdims=True)
        scaled = centered * lax.rsqrt(jnp.mean(centered * centered, axis=-1, keepdims=True) + 1e-06)
        modulated_s[block, :] = (scaled * (1.0 + scale_ref[...]) + shift_ref[...]).astype(jnp.bfloat16)
    latents = weight_ref.shape[0]
    diagonal = lax.broadcasted_iota(jnp.int32, (latents, latents), 0) == lax.broadcasted_iota(
        jnp.int32, (latents, latents), 1
    )
    bias = jnp.sum(jnp.where(diagonal, bias_ref[...], 0.0), axis=1, keepdims=True)
    velocity = (
        lax.dot_general(
            weight_ref[...], modulated_s[...], (((1,), (1,)), ((), ())), preferred_element_type=jnp.float32
        )
        + bias
    )
    tile = tile_ref[0]
    tile_row = tile // GRID_X
    tile_col = tile - tile_row * GRID_X
    live = (local_ref[0:1, :] < size_ref[0] - tile_row * TILE_H) & (local_ref[1:2, :] < size_ref[1] - tile_col * TILE_W)
    velocity = jnp.where(live, velocity, 0.0)
    area = jnp.full((1, PIX), size_ref[0] * size_ref[1], jnp.int32).astype(jnp.float32)
    moment = jnp.full((1, PIX), timestep_ref[0], jnp.int32).astype(jnp.float32)
    shift_factor = jnp.exp(0.5 + 0.65 * (area - 256.0) / 3840.0)
    now_time = 1.0 - moment / STEPS
    next_time = 1.0 - (moment + 1.0) / STEPS

    def sigma_of(at):
        return shift_factor * at / (shift_factor * at + 1.0 - at)

    step = sigma_of(next_time) - sigma_of(now_time)
    velocity_ref[...] = velocity
    next_ref[...] = latent_ref[...] + step * velocity


SMEM = pl.BlockSpec(memory_space=pltpu.SMEM)
VMEM = pl.BlockSpec(memory_space=pltpu.VMEM)
HBM = pl.BlockSpec(memory_space=pltpu.HBM)


def params(mebibytes):
    return pltpu.CompilerParams(vmem_limit_bytes=mebibytes * 1024 * 1024)


def shards(
    image_qkv,
    text_kv,
    q_gain,
    k_gain,
    out_weight,
    hidden,
    mlp_term,
    gate,
    final_shift,
    final_scale,
    final_weight,
    final_bias,
    latent,
    image_size,
    text_len,
    timestep,
):
    bf16 = jnp.bfloat16
    width = GROUP * HEAD
    model = hidden.shape[2]
    latents = final_weight.shape[1]
    tile = lax.axis_index("tile").astype(jnp.int32).reshape(1)
    kind = lax.axis_index("tp").astype(jnp.int32)
    which = jnp.where(kind == 0, tile[0] // GROUP, tile[0] % GRID_X // 2)
    group = jnp.stack([2 * kind + which, 2 * kind + 1 - which])
    triple = image_qkv.reshape(PIX, 3, width).transpose(1, 0, 2)
    kinds, partners = group_tiles()
    mesh_axes = ("tile", "tp")
    groups = [[int(t) * 2 + kind for t in tiles] for kind in range(2) for tiles in kinds[kind]]
    across = [(t * 2 + kind, int(partners[kind, t]) * 2 + kind) for t in range(TILES) for kind in range(2)]

    per_step = 2
    wide = per_step * HEAD
    rope = jnp.asarray(rope_tables())

    def slab(index):
        return pl.BlockSpec((1, PIX, wide), lambda i, tile_ref: (index, 0, i))

    gain_spec = pl.BlockSpec((1, HEAD), lambda i, tile_ref: (0, 0))
    rope_spec = pl.BlockSpec((1, 2, PIX, HEAD), lambda i, tile_ref: (tile_ref[0], 0, 0, 0))
    key_value = pl.pallas_call(
        key_value_kernel,
        grid_spec=pltpu.PrefetchScalarGridSpec(
            num_scalar_prefetch=1,
            grid=(GROUP // per_step,),
            in_specs=[
                slab(1),
                slab(2),
                pl.BlockSpec((SLOTS, 2, wide), lambda i, tile_ref: (0, 0, i)),
                gain_spec,
                rope_spec,
            ],
            out_specs=pl.BlockSpec((per_step, 2 * KEYS, HEAD), lambda i, tile_ref: (i, 0, 0)),
        ),
        out_shape=jax.ShapeDtypeStruct((GROUP, 2 * KEYS, HEAD), bf16),
        name="prepare_keys",
    )(tile, triple, triple, text_kv, k_gain.reshape(1, HEAD), rope)
    own = lax.all_to_all(key_value, mesh_axes, 0, 0, axis_index_groups=groups, tiled=True)
    queries = pl.pallas_call(
        query_kernel,
        grid_spec=pltpu.PrefetchScalarGridSpec(
            num_scalar_prefetch=1,
            grid=(GROUP // per_step,),
            in_specs=[slab(0), gain_spec, rope_spec],
            out_specs=pl.BlockSpec((per_step, PIX, HEAD), lambda i, tile_ref: (i, 0, 0)),
        ),
        out_shape=jax.ShapeDtypeStruct((GROUP, PIX, HEAD), bf16),
        name="prepare_queries",
    )(tile, triple, q_gain.reshape(1, HEAD), rope)
    own, queries = lax.optimization_barrier((own, queries))
    far = lax.ppermute(own, mesh_axes, across)
    queries = lax.all_to_all(queries, mesh_axes, 0, 0, axis_index_groups=groups, tiled=True)

    table = jnp.asarray(key_tables())
    acc, peak = pl.pallas_call(
        local_kernel,
        in_specs=[SMEM, SMEM, SMEM] + [VMEM] * 3,
        out_specs=(VMEM, VMEM),
        out_shape=(
            jax.ShapeDtypeStruct((GROUP, PIX, 2 * HEAD), jnp.float32),
            jax.ShapeDtypeStruct((GROUP, PIX, HEAD), jnp.float32),
        ),
        scratch_shapes=[pltpu.VMEM((HALF_KEYS, HEAD), bf16), pltpu.VMEM((HALF_KEYS, 2 * HEAD), bf16)],
        compiler_params=params(16),
        name="attend_local",
    )(group, image_size, text_len, table, queries, own)
    attended = pl.pallas_call(
        remote_kernel,
        in_specs=[SMEM, SMEM, SMEM] + [VMEM] * 5,
        out_specs=VMEM,
        out_shape=jax.ShapeDtypeStruct((GROUP, PIX, HEAD), bf16),
        scratch_shapes=[pltpu.VMEM((HALF_KEYS, HEAD), bf16), pltpu.VMEM((HALF_KEYS, 2 * HEAD), bf16)],
        compiler_params=params(16),
        name="attend_far",
    )(group, image_size, text_len, table, queries, far, acc, peak)
    attended = lax.all_to_all(attended, mesh_axes, 0, 0, axis_index_groups=groups, tiled=True)

    residual = pl.pallas_call(
        residual_kernel,
        in_specs=[VMEM, VMEM, VMEM],
        out_specs=VMEM,
        out_shape=jax.ShapeDtypeStruct((PIX, model), jnp.float32),
        compiler_params=params(8),
        name="residual",
    )(hidden.reshape(PIX, model), mlp_term.reshape(PIX, model), gate.reshape(1, model))
    attended, residual = lax.optimization_barrier((attended, residual))
    partial = pl.pallas_call(
        project_kernel,
        in_specs=[VMEM, VMEM],
        out_specs=VMEM,
        out_shape=jax.ShapeDtypeStruct((PIX, model), bf16),
        compiler_params=params(12),
        name="project",
    )(attended, out_weight)
    other = lax.ppermute(partial, "tp", [(0, 1), (1, 0)])

    local = np.stack([np.arange(PIX) // TILE_W, np.arange(PIX) % TILE_W]).astype(np.int32)
    velocity, latent_next = pl.pallas_call(
        final_kernel,
        in_specs=[SMEM, SMEM, SMEM] + [VMEM] * 10,
        out_specs=(VMEM, VMEM),
        out_shape=(jax.ShapeDtypeStruct((latents, PIX), jnp.float32),) * 2,
        scratch_shapes=[pltpu.VMEM((PIX, model), bf16)],
        compiler_params=params(12),
        name="final_layer",
    )(
        tile,
        image_size,
        timestep,
        jnp.asarray(local),
        partial,
        other,
        residual,
        gate.reshape(1, model),
        final_shift.reshape(1, model),
        final_scale.reshape(1, model),
        final_weight.T,
        final_bias.reshape(1, latents),
        latent.reshape(PIX, latents).T,
    )
    return (velocity.T.reshape(1, PIX, latents), latent_next.T.reshape(1, PIX, latents))


def solution(mesh):
    placed = (
        P(("req", "tile"), None, None, "tp"),
        P(("req", "tile"), None, "tp"),
        P(),
        P(),
        P("tp", None),
        P(("req", "tile"), None, None),
        P(("req", "tile"), None, None),
        P("req"),
        P("req"),
        P("req"),
        P(),
        P(),
        P(("req", "tile"), None, None),
        P("req"),
        P("req"),
        P("req"),
    )
    return jax.shard_map(
        shards,
        mesh=mesh,
        in_specs=placed,
        out_specs=(P(("req", "tile"), None, None), P(("req", "tile"), None, None)),
        check_vma=False,
    )
```

```python
import math

import jax
import jax.numpy as jnp
import numpy as np
from jax import lax
from jax.experimental import pallas as pl
from jax.experimental.pallas import tpu as pltpu
from jax.sharding import PartitionSpec as P

HEAD = 128
STEPS = 28
CANVAS = 48
TILES = 16
GRID_X = 4
TILE_H = 12
TILE_W = 12
PIX = TILE_H * TILE_W
SLOTS = 32
KEYS = PIX + SLOTS
GROUP = 8
HALF_KEYS = GROUP * KEYS
DEAD = -1e30
EXP_SCALE = HEAD ** (-0.5) * math.log2(math.e)


def position_tables():
    tile = np.arange(TILES)[:, None]
    local = np.arange(PIX)[None, :]
    row = tile // GRID_X * TILE_H + local // TILE_W
    col = tile % GRID_X * TILE_W + local % TILE_W
    return row, col


def rope_tables():
    row, col = position_tables()
    side_dims = (HEAD - HEAD // 8) // 2
    side_index = np.arange(side_dims // 2, dtype=np.float32)
    frequency = np.power(np.float32(10000.0), np.float32(-2.0) * side_index / np.float32(side_dims)).astype(np.float32)
    still = np.zeros(row.shape + (HEAD // 16,), np.float32)
    angles = np.concatenate(
        [
            still,
            row[..., None].astype(np.float32) * frequency,
            col[..., None].astype(np.float32) * frequency,
        ],
        axis=-1,
    ).astype(np.float64)
    cosine = np.repeat(np.cos(angles), 2, axis=-1)
    sine = np.repeat(np.sin(angles), 2, axis=-1)
    sine[..., 0::2] *= -1.0
    return np.stack([cosine, sine], axis=1).astype(np.float32)


def group_tiles():
    lows = np.arange(TILES // GRID_X)[:, None] * GRID_X
    kinds = [
        [np.arange(GROUP), np.arange(GROUP) + GROUP],
        [(lows + np.array([0, 1])).reshape(-1), (lows + np.array([3, 2])).reshape(-1)],
    ]
    partners = np.zeros((2, TILES), np.int64)
    for kind, (near, far) in enumerate(kinds):
        partners[kind, near] = far
        partners[kind, far] = near
    return kinds, partners


def key_tables():
    row, col = position_tables()
    far = np.full((GROUP, SLOTS), 1 << 20)
    beyond = np.full((GROUP, PIX), 1 << 20)
    tables = []
    for kind in group_tiles()[0]:
        for tiles in kind:
            slot = tiles[:, None] * SLOTS + np.arange(SLOTS)[None, :]
            parts = ((row[tiles], far), (col[tiles], far), (beyond, slot))
            tables.append(np.stack([np.concatenate(part, axis=1).reshape(HALF_KEYS) for part in parts]))
    return np.stack(tables).astype(np.int32)


def inverse_rms(vectors):
    wide = vectors.astype(jnp.float32)
    square = wide * wide
    high = square.astype(jnp.bfloat16)
    low = (square - high.astype(jnp.float32)).astype(jnp.bfloat16)
    ones = jnp.ones((2 * HEAD, HEAD), jnp.bfloat16)
    total = jnp.dot(jnp.concatenate([high, low], axis=1), ones, preferred_element_type=jnp.float32)
    return lax.rsqrt(total * (1.0 / HEAD) + 1e-06)


def swap_pairs(rows):
    even = lax.broadcasted_iota(jnp.int32, rows.shape, 1) % 2 == 0
    return jnp.where(even, pltpu.roll(rows, HEAD - 1, 1), pltpu.roll(rows, 1, 1))


def rotate_heads(source_ref, gain_ref, table_ref, out_ref):
    heads = out_ref.shape[0]
    gain = jnp.broadcast_to(gain_ref[...], (8, HEAD))
    along = table_ref[0, 0] * gain[0:1]
    across = table_ref[0, 1] * swap_pairs(gain)[0:1]
    stacked = jnp.concatenate([source_ref[0, :, h * HEAD : (h + 1) * HEAD] for h in range(heads)], axis=0)
    row = lax.broadcasted_iota(jnp.int32, (HEAD, HEAD), 0)
    col = lax.broadcasted_iota(jnp.int32, (HEAD, HEAD), 1)
    pairs = jnp.where(row + 1 - 2 * (row % 2) == col, 1.0, 0.0).astype(jnp.bfloat16)
    swapped = jnp.dot(stacked, pairs, preferred_element_type=jnp.float32)
    inverse = inverse_rms(stacked)
    for head in range(heads):
        rows = slice(head * PIX, (head + 1) * PIX)
        turned = stacked[rows].astype(jnp.float32) * along + swapped[rows] * across
        out_ref[head, 0:PIX, :] = (turned * inverse[rows]).astype(jnp.bfloat16)


def key_value_kernel(tile_ref, key_ref, value_ref, text_ref, gain_ref, table_ref, out_ref):
    rotate_heads(key_ref, gain_ref, table_ref, out_ref)
    text = text_ref[...]
    heads = out_ref.shape[0]
    text_keys = text[:, 0, :]
    text_values = text[:, 1, :]
    stacked = jnp.concatenate([text_keys[:, h * HEAD : (h + 1) * HEAD] for h in range(heads)], axis=0)
    text_keys = (stacked.astype(jnp.float32) * inverse_rms(stacked) * gain_ref[...]).astype(jnp.bfloat16)
    for head in range(heads):
        lanes = slice(head * HEAD, (head + 1) * HEAD)
        out_ref[head, PIX:KEYS, :] = text_keys[head * SLOTS : (head + 1) * SLOTS]
        out_ref[head, KEYS : KEYS + PIX, :] = value_ref[0, :, lanes]
        out_ref[head, KEYS + PIX :, :] = text_values[:, lanes]


def query_kernel(tile_ref, query_ref, gain_ref, table_ref, out_ref):
    rotate_heads(query_ref, gain_ref, table_ref, out_ref)


def key_bias(table_ref, size_ref, text_len_ref, group):
    image_ok = (table_ref[group, 0:1, :] < size_ref[0]) & (table_ref[group, 1:2, :] < size_ref[1])
    text_ok = table_ref[group, 2:3, :] < text_len_ref[0]
    return jnp.where(image_ok | text_ok, 0.0, DEAD)


def scores_of(queries, keys, bias):
    scores = lax.dot_general(queries, keys, (((1,), (1,)), ((), ())), preferred_element_type=jnp.float32)
    return scores + bias


def stage(source_ref, key_s, value_s):
    for tile in range(GROUP):
        rows = slice(tile * KEYS, (tile + 1) * KEYS)
        key_s[rows, :] = source_ref[tile, 0:KEYS, :]
        value_s[rows, 0:HEAD] = source_ref[tile, KEYS:, :]
    value_s[:, HEAD:] = jnp.ones((HALF_KEYS, HEAD), jnp.bfloat16)


def local_kernel(group_ref, size_ref, text_len_ref, table_ref, query_ref, own_ref, acc_ref, peak_ref, key_s, value_s):
    bias = key_bias(table_ref, size_ref, text_len_ref, group_ref[0])
    stage(own_ref, key_s, value_s)
    for tile in range(GROUP):
        scores = scores_of(query_ref[tile], key_s[...], bias)
        peak = jnp.max(scores, axis=1, keepdims=True)
        weights = jnp.exp2((scores - peak) * EXP_SCALE).astype(jnp.bfloat16)
        acc_ref[tile] = jnp.dot(weights, value_s[...], preferred_element_type=jnp.float32)
        peak_ref[tile] = jnp.broadcast_to(peak, (PIX, HEAD))


def remote_kernel(
    group_ref, size_ref, text_len_ref, table_ref, query_ref, far_ref, acc_ref, peak_ref, out_ref, key_s, value_s
):
    bias = key_bias(table_ref, size_ref, text_len_ref, group_ref[1])
    stage(far_ref, key_s, value_s)
    for tile in range(GROUP):
        scores = scores_of(query_ref[tile], key_s[...], bias)
        before = peak_ref[tile]
        peak = jnp.maximum(before[:, 0:1], jnp.max(scores, axis=1, keepdims=True))
        weights = jnp.exp2((scores - peak) * EXP_SCALE).astype(jnp.bfloat16)
        factor = jnp.exp2((before - peak) * EXP_SCALE)
        added = jnp.dot(weights, value_s[...], preferred_element_type=jnp.float32)
        blended = acc_ref[tile, :, 0:HEAD] * factor + added[:, 0:HEAD]
        total = acc_ref[tile, :, HEAD:] * factor + added[:, HEAD:]
        out_ref[tile] = (blended / total).astype(jnp.bfloat16)


def fetch_kernel(weight_ref, out_ref, sem):
    copy = pltpu.make_async_copy(weight_ref.at[:, pl.ds(0, out_ref.shape[1])], out_ref, sem)
    copy.start()
    copy.wait()


def project_kernel(attended_ref, ready_ref, weight_ref, out_ref, weight_s, sems):
    ready = ready_ref.shape[1]
    chunks = sems.shape[0]
    columns = weight_s.shape[1] // chunks
    copies = []
    for chunk in range(chunks):
        start = chunk * columns
        source = weight_ref.at[:, pl.ds(ready + start, columns)]
        copies.append(pltpu.make_async_copy(source, weight_s.at[:, pl.ds(start, columns)], sems.at[chunk]))
        copies[chunk].start()
    attended = jnp.concatenate([attended_ref[head] for head in range(GROUP)], axis=1)

    def projected(weight):
        return jnp.dot(attended, weight, preferred_element_type=jnp.float32).astype(jnp.bfloat16)

    out_ref[:, 0:ready] = projected(ready_ref[...])
    for chunk in range(chunks):
        start = chunk * columns
        copies[chunk].wait()
        out_ref[:, ready + start : ready + start + columns] = projected(weight_s[:, start : start + columns])


def final_kernel(
    tile_ref,
    size_ref,
    timestep_ref,
    local_ref,
    own_ref,
    other_ref,
    hidden_ref,
    mlp_ref,
    gate_ref,
    shift_ref,
    scale_ref,
    weight_ref,
    bias_ref,
    latent_ref,
    velocity_ref,
    next_ref,
    modulated_s,
):
    rows = 16
    for start in range(0, PIX, rows):
        block = slice(start, start + rows)
        projected = own_ref[block, :].astype(jnp.float32) + other_ref[block, :].astype(jnp.float32)
        state = hidden_ref[block, :].astype(jnp.float32) + gate_ref[...] * (
            projected + mlp_ref[block, :].astype(jnp.float32)
        )
        centered = state - jnp.mean(state, axis=-1, keepdims=True)
        scaled = centered * lax.rsqrt(jnp.mean(centered * centered, axis=-1, keepdims=True) + 1e-06)
        modulated_s[block, :] = (scaled * (1.0 + scale_ref[...]) + shift_ref[...]).astype(jnp.bfloat16)
    latents = weight_ref.shape[0]
    diagonal = lax.broadcasted_iota(jnp.int32, (latents, latents), 0) == lax.broadcasted_iota(
        jnp.int32, (latents, latents), 1
    )
    bias = jnp.sum(jnp.where(diagonal, bias_ref[...], 0.0), axis=1, keepdims=True)
    velocity = (
        lax.dot_general(
            weight_ref[...], modulated_s[...], (((1,), (1,)), ((), ())), preferred_element_type=jnp.float32
        )
        + bias
    )
    tile = tile_ref[0]
    tile_row = tile // GRID_X
    tile_col = tile - tile_row * GRID_X
    live = (local_ref[0:1, :] < size_ref[0] - tile_row * TILE_H) & (local_ref[1:2, :] < size_ref[1] - tile_col * TILE_W)
    velocity = jnp.where(live, velocity, 0.0)
    area = jnp.full((1, PIX), size_ref[0] * size_ref[1], jnp.int32).astype(jnp.float32)
    moment = jnp.full((1, PIX), timestep_ref[0], jnp.int32).astype(jnp.float32)
    shift_factor = jnp.exp(0.5 + 0.65 * (area - 256.0) / 3840.0)
    now_time = 1.0 - moment / STEPS
    next_time = 1.0 - (moment + 1.0) / STEPS

    def sigma_of(at):
        return shift_factor * at / (shift_factor * at + 1.0 - at)

    step = sigma_of(next_time) - sigma_of(now_time)
    velocity_ref[...] = velocity
    next_ref[...] = latent_ref[...] + step * velocity


SMEM = pl.BlockSpec(memory_space=pltpu.SMEM)
VMEM = pl.BlockSpec(memory_space=pltpu.VMEM)
HBM = pl.BlockSpec(memory_space=pltpu.HBM)


def params(mebibytes):
    return pltpu.CompilerParams(vmem_limit_bytes=mebibytes * 1024 * 1024)


def shards(
    image_qkv,
    text_kv,
    q_gain,
    k_gain,
    out_weight,
    hidden,
    mlp_term,
    gate,
    final_shift,
    final_scale,
    final_weight,
    final_bias,
    latent,
    image_size,
    text_len,
    timestep,
):
    bf16 = jnp.bfloat16
    width = GROUP * HEAD
    model = hidden.shape[2]
    latents = final_weight.shape[1]
    tile = lax.axis_index("tile").astype(jnp.int32).reshape(1)
    kind = lax.axis_index("tp").astype(jnp.int32)
    which = jnp.where(kind == 0, tile[0] // GROUP, tile[0] % GRID_X // 2)
    group = jnp.stack([2 * kind + which, 2 * kind + 1 - which])
    triple = image_qkv.reshape(PIX, 3, width).transpose(1, 0, 2)
    kinds, partners = group_tiles()
    mesh_axes = ("tile", "tp")
    groups = [[int(t) * 2 + kind for t in tiles] for kind in range(2) for tiles in kinds[kind]]
    across = [(t * 2 + kind, int(partners[kind, t]) * 2 + kind) for t in range(TILES) for kind in range(2)]

    per_step = 4
    wide = per_step * HEAD
    rope = jnp.asarray(rope_tables())

    def slab(index):
        return pl.BlockSpec((1, PIX, wide), lambda i, tile_ref: (index, 0, i))

    gain_spec = pl.BlockSpec((1, HEAD), lambda i, tile_ref: (0, 0))
    rope_spec = pl.BlockSpec((1, 2, PIX, HEAD), lambda i, tile_ref: (tile_ref[0], 0, 0, 0))
    key_value = pl.pallas_call(
        key_value_kernel,
        grid_spec=pltpu.PrefetchScalarGridSpec(
            num_scalar_prefetch=1,
            grid=(GROUP // per_step,),
            in_specs=[
                slab(1),
                slab(2),
                pl.BlockSpec((SLOTS, 2, wide), lambda i, tile_ref: (0, 0, i)),
                gain_spec,
                rope_spec,
            ],
            out_specs=pl.BlockSpec((per_step, 2 * KEYS, HEAD), lambda i, tile_ref: (i, 0, 0)),
        ),
        out_shape=jax.ShapeDtypeStruct((GROUP, 2 * KEYS, HEAD), bf16),
        name="prepare_keys",
    )(tile, triple, triple, text_kv, k_gain.reshape(1, HEAD), rope)
    own = lax.all_to_all(key_value, mesh_axes, 0, 0, axis_index_groups=groups, tiled=True)
    queries = pl.pallas_call(
        query_kernel,
        grid_spec=pltpu.PrefetchScalarGridSpec(
            num_scalar_prefetch=1,
            grid=(GROUP // per_step,),
            in_specs=[slab(0), gain_spec, rope_spec],
            out_specs=pl.BlockSpec((per_step, PIX, HEAD), lambda i, tile_ref: (i, 0, 0)),
        ),
        out_shape=jax.ShapeDtypeStruct((GROUP, PIX, HEAD), bf16),
        name="prepare_queries",
    )(tile, triple, q_gain.reshape(1, HEAD), rope)
    own, queries = lax.optimization_barrier((own, queries))
    far = lax.ppermute(own, mesh_axes, across)
    queries = lax.all_to_all(queries, mesh_axes, 0, 0, axis_index_groups=groups, tiled=True)

    table = jnp.asarray(key_tables())
    acc, peak = pl.pallas_call(
        local_kernel,
        in_specs=[SMEM, SMEM, SMEM] + [VMEM] * 3,
        out_specs=(VMEM, VMEM),
        out_shape=(
            jax.ShapeDtypeStruct((GROUP, PIX, 2 * HEAD), jnp.float32),
            jax.ShapeDtypeStruct((GROUP, PIX, HEAD), jnp.float32),
        ),
        scratch_shapes=[pltpu.VMEM((HALF_KEYS, HEAD), bf16), pltpu.VMEM((HALF_KEYS, 2 * HEAD), bf16)],
        compiler_params=params(16),
        name="attend_local",
    )(group, image_size, text_len, table, queries, own)
    attended = pl.pallas_call(
        remote_kernel,
        in_specs=[SMEM, SMEM, SMEM] + [VMEM] * 5,
        out_specs=VMEM,
        out_shape=jax.ShapeDtypeStruct((GROUP, PIX, HEAD), bf16),
        scratch_shapes=[pltpu.VMEM((HALF_KEYS, HEAD), bf16), pltpu.VMEM((HALF_KEYS, 2 * HEAD), bf16)],
        compiler_params=params(16),
        name="attend_far",
    )(group, image_size, text_len, table, queries, far, acc, peak)
    attended = lax.all_to_all(attended, mesh_axes, 0, 0, axis_index_groups=groups, tiled=True)

    ready = model // 2
    first_half = pl.pallas_call(
        fetch_kernel,
        in_specs=[HBM],
        out_specs=VMEM,
        out_shape=jax.ShapeDtypeStruct((width, ready), bf16),
        scratch_shapes=[pltpu.SemaphoreType.DMA],
        compiler_params=params(48),
        name="fetch_weight",
    )(out_weight)
    partial = pl.pallas_call(
        project_kernel,
        in_specs=[VMEM, VMEM, HBM],
        out_specs=VMEM,
        out_shape=jax.ShapeDtypeStruct((PIX, model), bf16),
        scratch_shapes=[pltpu.VMEM((width, model - ready), bf16), pltpu.SemaphoreType.DMA((3,))],
        compiler_params=params(48),
        name="project",
    )(attended, first_half, out_weight)
    other = lax.ppermute(partial, "tp", [(0, 1), (1, 0)])

    local = np.stack([np.arange(PIX) // TILE_W, np.arange(PIX) % TILE_W]).astype(np.int32)
    velocity, latent_next = pl.pallas_call(
        final_kernel,
        in_specs=[SMEM, SMEM, SMEM] + [VMEM] * 11,
        out_specs=(VMEM, VMEM),
        out_shape=(jax.ShapeDtypeStruct((latents, PIX), jnp.float32),) * 2,
        scratch_shapes=[pltpu.VMEM((PIX, model), bf16)],
        compiler_params=params(12),
        name="final_layer",
    )(
        tile,
        image_size,
        timestep,
        jnp.asarray(local),
        partial,
        other,
        hidden.reshape(PIX, model),
        mlp_term.reshape(PIX, model),
        gate.reshape(1, model),
        final_shift.reshape(1, model),
        final_scale.reshape(1, model),
        final_weight.T,
        final_bias.reshape(1, latents),
        latent.reshape(PIX, latents).T,
    )
    return (velocity.T.reshape(1, PIX, latents), latent_next.T.reshape(1, PIX, latents))


def solution(mesh):
    placed = (
        P(("req", "tile"), None, None, "tp"),
        P(("req", "tile"), None, "tp"),
        P(),
        P(),
        P("tp", None),
        P(("req", "tile"), None, None),
        P(("req", "tile"), None, None),
        P("req"),
        P("req"),
        P("req"),
        P(),
        P(),
        P(("req", "tile"), None, None),
        P("req"),
        P("req"),
        P("req"),
    )
    return jax.shard_map(
        shards,
        mesh=mesh,
        in_specs=placed,
        out_specs=(P(("req", "tile"), None, None), P(("req", "tile"), None, None)),
        check_vma=False,
    )
```

```python
import math

import jax
import jax.numpy as jnp
import numpy as np
from jax import lax
from jax.experimental import pallas as pl
from jax.experimental.pallas import tpu as pltpu
from jax.sharding import PartitionSpec as P

HEAD = 128
STEPS = 28
CANVAS = 48
TILES = 16
GRID_X = 4
TILE_H = 12
TILE_W = 12
PIX = TILE_H * TILE_W
SLOTS = 32
KEYS = PIX + SLOTS
GROUP = 8
HALF_KEYS = GROUP * KEYS
QUERIES = GROUP * PIX
QUERY_BLOCK = QUERIES // 2
FAR_BLOCK = QUERIES // 4
KEY_CHUNK = 256
READY = (1536,)
DEAD = -1e30
EXP_SCALE = HEAD ** (-0.5) * math.log2(math.e)


def position_tables():
    tile = np.arange(TILES)[:, None]
    local = np.arange(PIX)[None, :]
    row = tile // GRID_X * TILE_H + local // TILE_W
    col = tile % GRID_X * TILE_W + local % TILE_W
    return row, col


def rope_tables():
    row, col = position_tables()
    side_dims = (HEAD - HEAD // 8) // 2
    side_index = np.arange(side_dims // 2, dtype=np.float32)
    frequency = np.power(np.float32(10000.0), np.float32(-2.0) * side_index / np.float32(side_dims)).astype(np.float32)
    still = np.zeros(row.shape + (HEAD // 16,), np.float32)
    angles = np.concatenate(
        [
            still,
            row[..., None].astype(np.float32) * frequency,
            col[..., None].astype(np.float32) * frequency,
        ],
        axis=-1,
    ).astype(np.float64)
    cosine = np.repeat(np.cos(angles), 2, axis=-1)
    sine = np.repeat(np.sin(angles), 2, axis=-1)
    sine[..., 0::2] *= -1.0
    return np.stack([cosine, sine], axis=1).astype(np.float32)


def group_tiles():
    lows = np.arange(TILES // GRID_X)[:, None] * GRID_X
    kinds = [
        [np.arange(GROUP), np.arange(GROUP) + GROUP],
        [(lows + np.array([0, 1])).reshape(-1), (lows + np.array([3, 2])).reshape(-1)],
    ]
    partners = np.zeros((2, TILES), np.int64)
    for kind, (near, far) in enumerate(kinds):
        partners[kind, near] = far
        partners[kind, far] = near
    return kinds, partners


def key_tables():
    row, col = position_tables()
    far = np.full((GROUP, SLOTS), 1 << 20)
    beyond = np.full((GROUP, PIX), 1 << 20)
    tables = []
    for kind in group_tiles()[0]:
        for tiles in kind:
            slot = tiles[:, None] * SLOTS + np.arange(SLOTS)[None, :]
            parts = ((row[tiles], far), (col[tiles], far), (beyond, slot))
            tables.append(np.stack([np.concatenate(part, axis=1).reshape(HALF_KEYS) for part in parts]))
    return np.stack(tables).astype(np.int32)


def inverse_rms(vectors):
    wide = vectors.astype(jnp.float32)
    square = wide * wide
    high = square.astype(jnp.bfloat16)
    low = (square - high.astype(jnp.float32)).astype(jnp.bfloat16)
    ones = jnp.ones((2 * HEAD, HEAD), jnp.bfloat16)
    total = jnp.dot(jnp.concatenate([high, low], axis=1), ones, preferred_element_type=jnp.float32)
    return lax.rsqrt(total * (1.0 / HEAD) + 1e-06)


def swap_pairs(rows):
    even = lax.broadcasted_iota(jnp.int32, rows.shape, 1) % 2 == 0
    return jnp.where(even, pltpu.roll(rows, HEAD - 1, 1), pltpu.roll(rows, 1, 1))


def rotate_heads(source_ref, gain_ref, table_ref, out_ref):
    heads = out_ref.shape[0]
    gain = jnp.broadcast_to(gain_ref[...], (8, HEAD))
    along = table_ref[0, 0] * gain[0:1]
    across = table_ref[0, 1] * swap_pairs(gain)[0:1]
    stacked = jnp.concatenate([source_ref[0, :, h * HEAD : (h + 1) * HEAD] for h in range(heads)], axis=0)
    row = lax.broadcasted_iota(jnp.int32, (HEAD, HEAD), 0)
    col = lax.broadcasted_iota(jnp.int32, (HEAD, HEAD), 1)
    pairs = jnp.where(row + 1 - 2 * (row % 2) == col, 1.0, 0.0).astype(jnp.bfloat16)
    swapped = jnp.dot(stacked, pairs, preferred_element_type=jnp.float32)
    inverse = inverse_rms(stacked)
    for head in range(heads):
        rows = slice(head * PIX, (head + 1) * PIX)
        turned = stacked[rows].astype(jnp.float32) * along + swapped[rows] * across
        out_ref[head, 0:PIX, :] = (turned * inverse[rows]).astype(jnp.bfloat16)


def key_value_kernel(tile_ref, key_ref, value_ref, text_ref, gain_ref, table_ref, out_ref):
    rotate_heads(key_ref, gain_ref, table_ref, out_ref)
    text = text_ref[...]
    heads = out_ref.shape[0]
    text_keys = text[:, 0, :]
    text_values = text[:, 1, :]
    stacked = jnp.concatenate([text_keys[:, h * HEAD : (h + 1) * HEAD] for h in range(heads)], axis=0)
    text_keys = (stacked.astype(jnp.float32) * inverse_rms(stacked) * gain_ref[...]).astype(jnp.bfloat16)
    for head in range(heads):
        lanes = slice(head * HEAD, (head + 1) * HEAD)
        out_ref[head, PIX:KEYS, :] = text_keys[head * SLOTS : (head + 1) * SLOTS]
        out_ref[head, KEYS : KEYS + PIX, :] = value_ref[0, :, lanes]
        out_ref[head, KEYS + PIX :, :] = text_values[:, lanes]


def query_kernel(tile_ref, query_ref, gain_ref, table_ref, out_ref):
    rotate_heads(query_ref, gain_ref, table_ref, out_ref)


def key_bias(table_ref, size_ref, text_len_ref, group):
    image_ok = (table_ref[group, 0:1, :] < size_ref[0]) & (table_ref[group, 1:2, :] < size_ref[1])
    text_ok = table_ref[group, 2:3, :] < text_len_ref[0]
    return jnp.where(image_ok | text_ok, 0.0, DEAD)


def score_chunks(queries, key_s, bias):
    chunks = []
    for start in range(0, key_s.shape[0], KEY_CHUNK):
        part = slice(start, min(start + KEY_CHUNK, key_s.shape[0]))
        scores = lax.dot_general(
            queries, key_s[part, :], (((1,), (1,)), ((), ())), preferred_element_type=jnp.float32
        )
        chunks.append(scores + bias[:, part])
    return chunks


def peak_of(chunks):
    peak = jnp.max(chunks[0], axis=1, keepdims=True)
    for scores in chunks[1:]:
        peak = jnp.maximum(peak, jnp.max(scores, axis=1, keepdims=True))
    return peak


def weighted(chunks, peak, value_s):
    blended = None
    start = 0
    for scores in chunks:
        stop = start + scores.shape[1]
        weights = jnp.exp2((scores - peak) * EXP_SCALE).astype(jnp.bfloat16)
        added = jnp.dot(weights, value_s[start:stop, :], preferred_element_type=jnp.float32)
        blended = added if blended is None else blended + added
        start = stop
    return blended


def stage(source_ref, key_s, value_s):
    for tile in range(GROUP):
        rows = slice(tile * KEYS, (tile + 1) * KEYS)
        key_s[rows, :] = source_ref[tile, 0:KEYS, :]
        value_s[rows, 0:HEAD] = source_ref[tile, KEYS:, :]
    value_s[:, HEAD:] = jnp.ones((HALF_KEYS, HEAD), jnp.bfloat16)


def local_kernel(
    group_ref, size_ref, text_len_ref, table_ref, query_ref, own_ref, acc_ref, peak_ref, key_s, value_s
):
    bias = key_bias(table_ref, size_ref, text_len_ref, group_ref[0])
    stage(own_ref, key_s, value_s)
    for start in range(0, QUERIES, QUERY_BLOCK):
        block = slice(start, start + QUERY_BLOCK)
        chunks = score_chunks(query_ref[block, :], key_s, bias)
        peak = peak_of(chunks)
        acc_ref[block, :] = weighted(chunks, peak, value_s)
        peak_ref[block, :] = jnp.broadcast_to(peak, (QUERY_BLOCK, HEAD))


def remote_kernel(
    group_ref, size_ref, text_len_ref, table_ref, query_ref, far_ref, acc_ref, peak_ref, out_ref, key_s, value_s
):
    bias = key_bias(table_ref, size_ref, text_len_ref, group_ref[1])
    stage(far_ref, key_s, value_s)
    blocks = [slice(start, start + FAR_BLOCK) for start in range(0, QUERIES, FAR_BLOCK)]
    ahead = score_chunks(query_ref[blocks[0], :], key_s, bias)
    for index, block in enumerate(blocks):
        chunks = ahead
        if index + 1 < len(blocks):
            ahead = score_chunks(query_ref[blocks[index + 1], :], key_s, bias)
        before = peak_ref[block, :]
        peak = jnp.maximum(before[:, 0:1], peak_of(chunks))
        factor = jnp.exp2((before - peak) * EXP_SCALE)
        added = weighted(chunks, peak, value_s)
        blended = acc_ref[block, 0:HEAD] * factor + added[:, 0:HEAD]
        total = acc_ref[block, HEAD:] * factor + added[:, HEAD:]
        out_ref[block, :] = (blended / total).astype(jnp.bfloat16)


def fetch_kernel(weight_ref, *refs):
    sems = refs[-1]
    copies = []
    start = 0
    for index, part_ref in enumerate(refs[:-1]):
        columns = part_ref.shape[1]
        copies.append(pltpu.make_async_copy(weight_ref.at[:, pl.ds(start, columns)], part_ref, sems.at[index]))
        copies[index].start()
        start += columns
    for copy in copies:
        copy.wait()


def project_kernel(attended_ref, *refs):
    ready_refs = refs[: len(READY)]
    weight_ref, out_ref, weight_s, sems = refs[len(READY) :]
    chunks = sems.shape[0]
    columns = weight_s.shape[1] // chunks
    copies = []
    for chunk in range(chunks):
        part = pl.ds(chunk * columns, columns)
        source = weight_ref.at[:, pl.ds(sum(READY) + chunk * columns, columns)]
        copies.append(pltpu.make_async_copy(source, weight_s.at[:, part], sems.at[chunk]))
        copies[chunk].start()
    attended = jnp.concatenate([attended_ref[head] for head in range(GROUP)], axis=1)

    def projected(weight):
        return jnp.dot(attended, weight, preferred_element_type=jnp.float32).astype(jnp.bfloat16)

    start = 0
    for ready_ref in ready_refs:
        out_ref[:, start : start + ready_ref.shape[1]] = projected(ready_ref[...])
        start += ready_ref.shape[1]
    for chunk in range(chunks):
        copies[chunk].wait()
        out_ref[:, start : start + columns] = projected(weight_s[:, chunk * columns : (chunk + 1) * columns])
        start += columns


def final_kernel(
    tile_ref,
    size_ref,
    timestep_ref,
    local_ref,
    own_ref,
    other_ref,
    hidden_ref,
    mlp_ref,
    gate_ref,
    shift_ref,
    scale_ref,
    weight_ref,
    bias_ref,
    latent_ref,
    velocity_ref,
    next_ref,
    modulated_s,
):
    rows = 16
    for start in range(0, PIX, rows):
        block = slice(start, start + rows)
        projected = own_ref[block, :].astype(jnp.float32) + other_ref[block, :].astype(jnp.float32)
        state = hidden_ref[block, :].astype(jnp.float32) + gate_ref[...] * (
            projected + mlp_ref[block, :].astype(jnp.float32)
        )
        centered = state - jnp.mean(state, axis=-1, keepdims=True)
        scaled = centered * lax.rsqrt(jnp.mean(centered * centered, axis=-1, keepdims=True) + 1e-06)
        modulated_s[block, :] = (scaled * (1.0 + scale_ref[...]) + shift_ref[...]).astype(jnp.bfloat16)
    latents = weight_ref.shape[0]
    diagonal = lax.broadcasted_iota(jnp.int32, (latents, latents), 0) == lax.broadcasted_iota(
        jnp.int32, (latents, latents), 1
    )
    bias = jnp.sum(jnp.where(diagonal, bias_ref[...], 0.0), axis=1, keepdims=True)
    velocity = (
        lax.dot_general(
            weight_ref[...], modulated_s[...], (((1,), (1,)), ((), ())), preferred_element_type=jnp.float32
        )
        + bias
    )
    tile = tile_ref[0]
    tile_row = tile // GRID_X
    tile_col = tile - tile_row * GRID_X
    live = (local_ref[0:1, :] < size_ref[0] - tile_row * TILE_H) & (local_ref[1:2, :] < size_ref[1] - tile_col * TILE_W)
    velocity = jnp.where(live, velocity, 0.0)
    area = jnp.full((1, PIX), size_ref[0] * size_ref[1], jnp.int32).astype(jnp.float32)
    moment = jnp.full((1, PIX), timestep_ref[0], jnp.int32).astype(jnp.float32)
    shift_factor = jnp.exp(0.5 + 0.65 * (area - 256.0) / 3840.0)
    now_time = 1.0 - moment / STEPS
    next_time = 1.0 - (moment + 1.0) / STEPS

    def sigma_of(at):
        return shift_factor * at / (shift_factor * at + 1.0 - at)

    step = sigma_of(next_time) - sigma_of(now_time)
    velocity_ref[...] = velocity
    next_ref[...] = latent_ref[...] + step * velocity


SMEM = pl.BlockSpec(memory_space=pltpu.SMEM)
VMEM = pl.BlockSpec(memory_space=pltpu.VMEM)
HBM = pl.BlockSpec(memory_space=pltpu.HBM)


def params(mebibytes):
    return pltpu.CompilerParams(vmem_limit_bytes=mebibytes * 1024 * 1024)


def shards(
    image_qkv,
    text_kv,
    q_gain,
    k_gain,
    out_weight,
    hidden,
    mlp_term,
    gate,
    final_shift,
    final_scale,
    final_weight,
    final_bias,
    latent,
    image_size,
    text_len,
    timestep,
):
    bf16 = jnp.bfloat16
    width = GROUP * HEAD
    model = hidden.shape[2]
    latents = final_weight.shape[1]
    tile = lax.axis_index("tile").astype(jnp.int32).reshape(1)
    kind = lax.axis_index("tp").astype(jnp.int32)
    which = jnp.where(kind == 0, tile[0] // GROUP, tile[0] % GRID_X // 2)
    group = jnp.stack([2 * kind + which, 2 * kind + 1 - which])
    triple = image_qkv.reshape(PIX, 3, width).transpose(1, 0, 2)
    kinds, partners = group_tiles()
    mesh_axes = ("tile", "tp")
    groups = [[int(t) * 2 + kind for t in tiles] for kind in range(2) for tiles in kinds[kind]]
    across = [(t * 2 + kind, int(partners[kind, t]) * 2 + kind) for t in range(TILES) for kind in range(2)]

    per_step = 8
    wide = per_step * HEAD
    rope = jnp.asarray(rope_tables())

    def slab(index):
        return pl.BlockSpec((1, PIX, wide), lambda i, tile_ref: (index, 0, i))

    gain_spec = pl.BlockSpec((1, HEAD), lambda i, tile_ref: (0, 0))
    rope_spec = pl.BlockSpec((1, 2, PIX, HEAD), lambda i, tile_ref: (tile_ref[0], 0, 0, 0))
    key_value = pl.pallas_call(
        key_value_kernel,
        grid_spec=pltpu.PrefetchScalarGridSpec(
            num_scalar_prefetch=1,
            grid=(GROUP // per_step,),
            in_specs=[
                slab(1),
                slab(2),
                pl.BlockSpec((SLOTS, 2, wide), lambda i, tile_ref: (0, 0, i)),
                gain_spec,
                rope_spec,
            ],
            out_specs=pl.BlockSpec((per_step, 2 * KEYS, HEAD), lambda i, tile_ref: (i, 0, 0)),
        ),
        out_shape=jax.ShapeDtypeStruct((GROUP, 2 * KEYS, HEAD), bf16),
        name="prepare_keys",
    )(tile, triple, triple, text_kv, k_gain.reshape(1, HEAD), rope)
    own = lax.all_to_all(key_value, mesh_axes, 0, 0, axis_index_groups=groups, tiled=True)
    queries = pl.pallas_call(
        query_kernel,
        grid_spec=pltpu.PrefetchScalarGridSpec(
            num_scalar_prefetch=1,
            grid=(GROUP // per_step,),
            in_specs=[slab(0), gain_spec, rope_spec],
            out_specs=pl.BlockSpec((per_step, PIX, HEAD), lambda i, tile_ref: (i, 0, 0)),
        ),
        out_shape=jax.ShapeDtypeStruct((GROUP, PIX, HEAD), bf16),
        name="prepare_queries",
    )(tile, triple, q_gain.reshape(1, HEAD), rope)
    own, queries = lax.optimization_barrier((own, queries))
    far = lax.ppermute(own, mesh_axes, across)
    queries = lax.all_to_all(queries, mesh_axes, 0, 0, axis_index_groups=groups, tiled=True)

    queries = queries.reshape(QUERIES, HEAD)
    table = jnp.asarray(key_tables())
    acc, peak = pl.pallas_call(
        local_kernel,
        in_specs=[SMEM, SMEM, SMEM] + [VMEM] * 3,
        out_specs=(VMEM, VMEM),
        out_shape=(
            jax.ShapeDtypeStruct((QUERIES, 2 * HEAD), jnp.float32),
            jax.ShapeDtypeStruct((QUERIES, HEAD), jnp.float32),
        ),
        scratch_shapes=[pltpu.VMEM((HALF_KEYS, HEAD), bf16), pltpu.VMEM((HALF_KEYS, 2 * HEAD), bf16)],
        compiler_params=params(16),
        name="attend_local",
    )(group, image_size, text_len, table, queries, own)
    attended = pl.pallas_call(
        remote_kernel,
        in_specs=[SMEM, SMEM, SMEM] + [VMEM] * 5,
        out_specs=VMEM,
        out_shape=jax.ShapeDtypeStruct((QUERIES, HEAD), bf16),
        scratch_shapes=[pltpu.VMEM((HALF_KEYS, HEAD), bf16), pltpu.VMEM((HALF_KEYS, 2 * HEAD), bf16)],
        compiler_params=params(16),
        name="attend_far",
    )(group, image_size, text_len, table, queries, far, acc, peak)
    attended = attended.reshape(GROUP, PIX, HEAD)
    attended = lax.all_to_all(attended, mesh_axes, 0, 0, axis_index_groups=groups, tiled=True)

    ready = pl.pallas_call(
        fetch_kernel,
        in_specs=[HBM],
        out_specs=(VMEM,) * len(READY),
        out_shape=tuple(jax.ShapeDtypeStruct((width, columns), bf16) for columns in READY),
        scratch_shapes=[pltpu.SemaphoreType.DMA((len(READY),))],
        compiler_params=params(48),
        name="fetch_weight",
    )(out_weight)
    partial = pl.pallas_call(
        project_kernel,
        in_specs=[VMEM] * (1 + len(READY)) + [HBM],
        out_specs=VMEM,
        out_shape=jax.ShapeDtypeStruct((PIX, model), bf16),
        scratch_shapes=[pltpu.VMEM((width, model - sum(READY)), bf16), pltpu.SemaphoreType.DMA((2,))],
        compiler_params=params(48),
        name="project",
    )(attended, *ready, out_weight)
    other = lax.ppermute(partial, "tp", [(0, 1), (1, 0)])

    local = np.stack([np.arange(PIX) // TILE_W, np.arange(PIX) % TILE_W]).astype(np.int32)
    velocity, latent_next = pl.pallas_call(
        final_kernel,
        in_specs=[SMEM, SMEM, SMEM] + [VMEM] * 11,
        out_specs=(VMEM, VMEM),
        out_shape=(jax.ShapeDtypeStruct((latents, PIX), jnp.float32),) * 2,
        scratch_shapes=[pltpu.VMEM((PIX, model), bf16)],
        compiler_params=params(12),
        name="final_layer",
    )(
        tile,
        image_size,
        timestep,
        jnp.asarray(local),
        partial,
        other,
        hidden.reshape(PIX, model),
        mlp_term.reshape(PIX, model),
        gate.reshape(1, model),
        final_shift.reshape(1, model),
        final_scale.reshape(1, model),
        final_weight.T,
        final_bias.reshape(1, latents),
        latent.reshape(PIX, latents).T,
    )
    return (velocity.T.reshape(1, PIX, latents), latent_next.T.reshape(1, PIX, latents))


def solution(mesh):
    placed = (
        P(("req", "tile"), None, None, "tp"),
        P(("req", "tile"), None, "tp"),
        P(),
        P(),
        P("tp", None),
        P(("req", "tile"), None, None),
        P(("req", "tile"), None, None),
        P("req"),
        P("req"),
        P("req"),
        P(),
        P(),
        P(("req", "tile"), None, None),
        P("req"),
        P("req"),
        P("req"),
    )
    return jax.shard_map(
        shards,
        mesh=mesh,
        in_specs=placed,
        out_specs=(P(("req", "tile"), None, None), P(("req", "tile"), None, None)),
        check_vma=False,
    )
```

```python
import math

import jax
import jax.numpy as jnp
import numpy as np
from jax import lax
from jax.experimental import pallas as pl
from jax.experimental.pallas import tpu as pltpu
from jax.sharding import PartitionSpec as P

HEAD = 128
STEPS = 28
CANVAS = 48
TILES = 16
GRID_X = 4
TILE_H = 12
TILE_W = 12
PIX = TILE_H * TILE_W
SLOTS = 32
KEYS = PIX + SLOTS
GROUP = 8
HALF_KEYS = GROUP * KEYS
QUERIES = GROUP * PIX
QUERY_BLOCK = QUERIES // 2
FAR_BLOCK = QUERIES // 4
KEY_CHUNK = 256
READY = (1536,)
DEAD = -1e30
EXP_SCALE = HEAD ** (-0.5) * math.log2(math.e)


def position_tables():
    tile = np.arange(TILES)[:, None]
    local = np.arange(PIX)[None, :]
    row = tile // GRID_X * TILE_H + local // TILE_W
    col = tile % GRID_X * TILE_W + local % TILE_W
    return row, col


def rope_tables():
    row, col = position_tables()
    side_dims = (HEAD - HEAD // 8) // 2
    side_index = np.arange(side_dims // 2, dtype=np.float32)
    frequency = np.power(np.float32(10000.0), np.float32(-2.0) * side_index / np.float32(side_dims)).astype(np.float32)
    still = np.zeros(row.shape + (HEAD // 16,), np.float32)
    angles = np.concatenate(
        [
            still,
            row[..., None].astype(np.float32) * frequency,
            col[..., None].astype(np.float32) * frequency,
        ],
        axis=-1,
    ).astype(np.float64)
    cosine = np.repeat(np.cos(angles), 2, axis=-1)
    sine = np.repeat(np.sin(angles), 2, axis=-1)
    sine[..., 0::2] *= -1.0
    return np.stack([cosine, sine], axis=1).astype(np.float32)


def group_tiles():
    lows = np.arange(TILES // GRID_X)[:, None] * GRID_X
    kinds = [
        [(lows + np.array([0, 1])).reshape(-1), (lows + np.array([3, 2])).reshape(-1)],
        [np.arange(GROUP), np.arange(GROUP) + GROUP],
    ]
    partners = np.zeros((2, TILES), np.int64)
    for kind, (near, far) in enumerate(kinds):
        partners[kind, near] = far
        partners[kind, far] = near
    return kinds, partners


def key_tables():
    row, col = position_tables()
    far = np.full((GROUP, SLOTS), 1 << 20)
    beyond = np.full((GROUP, PIX), 1 << 20)
    tables = []
    for kind in group_tiles()[0]:
        for tiles in kind:
            slot = tiles[:, None] * SLOTS + np.arange(SLOTS)[None, :]
            parts = ((row[tiles], far), (col[tiles], far), (beyond, slot))
            tables.append(np.stack([np.concatenate(part, axis=1).reshape(HALF_KEYS) for part in parts]))
    return np.stack(tables).astype(np.int32)


def inverse_rms(vectors):
    wide = vectors.astype(jnp.float32)
    square = wide * wide
    high = square.astype(jnp.bfloat16)
    low = (square - high.astype(jnp.float32)).astype(jnp.bfloat16)
    ones = jnp.ones((2 * HEAD, HEAD), jnp.bfloat16)
    total = jnp.dot(jnp.concatenate([high, low], axis=1), ones, preferred_element_type=jnp.float32)
    return lax.rsqrt(total * (1.0 / HEAD) + 1e-06)


def swap_pairs(rows):
    even = lax.broadcasted_iota(jnp.int32, rows.shape, 1) % 2 == 0
    return jnp.where(even, pltpu.roll(rows, HEAD - 1, 1), pltpu.roll(rows, 1, 1))


def rotate_heads(source_ref, gain_ref, table_ref, out_ref):
    heads = out_ref.shape[0]
    gain = jnp.broadcast_to(gain_ref[...], (8, HEAD))
    along = table_ref[0, 0] * gain[0:1]
    across = table_ref[0, 1] * swap_pairs(gain)[0:1]
    stacked = jnp.concatenate([source_ref[0, :, h * HEAD : (h + 1) * HEAD] for h in range(heads)], axis=0)
    row = lax.broadcasted_iota(jnp.int32, (HEAD, HEAD), 0)
    col = lax.broadcasted_iota(jnp.int32, (HEAD, HEAD), 1)
    pairs = jnp.where(row + 1 - 2 * (row % 2) == col, 1.0, 0.0).astype(jnp.bfloat16)
    swapped = jnp.dot(stacked, pairs, preferred_element_type=jnp.float32)
    inverse = inverse_rms(stacked)
    for head in range(heads):
        rows = slice(head * PIX, (head + 1) * PIX)
        turned = stacked[rows].astype(jnp.float32) * along + swapped[rows] * across
        out_ref[head, 0:PIX, :] = (turned * inverse[rows]).astype(jnp.bfloat16)


def key_value_kernel(tile_ref, key_ref, value_ref, text_ref, gain_ref, table_ref, out_ref):
    rotate_heads(key_ref, gain_ref, table_ref, out_ref)
    text = text_ref[...]
    heads = out_ref.shape[0]
    text_keys = text[:, 0, :]
    text_values = text[:, 1, :]
    stacked = jnp.concatenate([text_keys[:, h * HEAD : (h + 1) * HEAD] for h in range(heads)], axis=0)
    text_keys = (stacked.astype(jnp.float32) * inverse_rms(stacked) * gain_ref[...]).astype(jnp.bfloat16)
    for head in range(heads):
        lanes = slice(head * HEAD, (head + 1) * HEAD)
        out_ref[head, PIX:KEYS, :] = text_keys[head * SLOTS : (head + 1) * SLOTS]
        out_ref[head, KEYS : KEYS + PIX, :] = value_ref[0, :, lanes]
        out_ref[head, KEYS + PIX :, :] = text_values[:, lanes]


def query_kernel(tile_ref, query_ref, gain_ref, table_ref, out_ref):
    rotate_heads(query_ref, gain_ref, table_ref, out_ref)


def key_bias(table_ref, size_ref, text_len_ref, group):
    image_ok = (table_ref[group, 0:1, :] < size_ref[0]) & (table_ref[group, 1:2, :] < size_ref[1])
    text_ok = table_ref[group, 2:3, :] < text_len_ref[0]
    return jnp.where(image_ok | text_ok, 0.0, DEAD)


def score_chunks(queries, key_s, bias):
    chunks = []
    for start in range(0, key_s.shape[0], KEY_CHUNK):
        part = slice(start, min(start + KEY_CHUNK, key_s.shape[0]))
        scores = lax.dot_general(
            queries, key_s[part, :], (((1,), (1,)), ((), ())), preferred_element_type=jnp.float32
        )
        chunks.append(scores + bias[:, part])
    return chunks


def peak_of(chunks):
    peak = jnp.max(chunks[0], axis=1, keepdims=True)
    for scores in chunks[1:]:
        peak = jnp.maximum(peak, jnp.max(scores, axis=1, keepdims=True))
    return peak


def weighted(chunks, peak, value_s):
    blended = None
    start = 0
    for scores in chunks:
        stop = start + scores.shape[1]
        weights = jnp.exp2((scores - peak) * EXP_SCALE).astype(jnp.bfloat16)
        added = jnp.dot(weights, value_s[start:stop, :], preferred_element_type=jnp.float32)
        blended = added if blended is None else blended + added
        start = stop
    return blended


def stage(source_ref, key_s, value_s):
    for tile in range(GROUP):
        rows = slice(tile * KEYS, (tile + 1) * KEYS)
        key_s[rows, :] = source_ref[tile, 0:KEYS, :]
        value_s[rows, 0:HEAD] = source_ref[tile, KEYS:, :]
    value_s[:, HEAD:] = jnp.ones((HALF_KEYS, HEAD), jnp.bfloat16)


def local_kernel(
    group_ref, size_ref, text_len_ref, table_ref, query_ref, own_ref, acc_ref, peak_ref, key_s, value_s
):
    bias = key_bias(table_ref, size_ref, text_len_ref, group_ref[0])
    stage(own_ref, key_s, value_s)
    for start in range(0, QUERIES, QUERY_BLOCK):
        block = slice(start, start + QUERY_BLOCK)
        chunks = score_chunks(query_ref[block, :], key_s, bias)
        peak = peak_of(chunks)
        acc_ref[block, :] = weighted(chunks, peak, value_s)
        peak_ref[block, :] = jnp.broadcast_to(peak, (QUERY_BLOCK, HEAD))


def remote_kernel(
    group_ref, size_ref, text_len_ref, table_ref, query_ref, far_ref, acc_ref, peak_ref, out_ref, key_s, value_s
):
    bias = key_bias(table_ref, size_ref, text_len_ref, group_ref[1])
    stage(far_ref, key_s, value_s)
    blocks = [slice(start, start + FAR_BLOCK) for start in range(0, QUERIES, FAR_BLOCK)]
    ahead = score_chunks(query_ref[blocks[0], :], key_s, bias)
    for index, block in enumerate(blocks):
        chunks = ahead
        if index + 1 < len(blocks):
            ahead = score_chunks(query_ref[blocks[index + 1], :], key_s, bias)
        before = peak_ref[block, :]
        peak = jnp.maximum(before[:, 0:1], peak_of(chunks))
        factor = jnp.exp2((before - peak) * EXP_SCALE)
        added = weighted(chunks, peak, value_s)
        blended = acc_ref[block, 0:HEAD] * factor + added[:, 0:HEAD]
        total = acc_ref[block, HEAD:] * factor + added[:, HEAD:]
        out_ref[block, :] = (blended / total).astype(jnp.bfloat16)


def fetch_kernel(weight_ref, *refs):
    sems = refs[-1]
    copies = []
    start = 0
    for index, part_ref in enumerate(refs[:-1]):
        columns = part_ref.shape[1]
        copies.append(pltpu.make_async_copy(weight_ref.at[:, pl.ds(start, columns)], part_ref, sems.at[index]))
        copies[index].start()
        start += columns
    for copy in copies:
        copy.wait()


def project_kernel(attended_ref, *refs):
    ready_refs = refs[: len(READY)]
    weight_ref, out_ref, weight_s, sems = refs[len(READY) :]
    chunks = sems.shape[0]
    columns = weight_s.shape[1] // chunks
    copies = []
    for chunk in range(chunks):
        part = pl.ds(chunk * columns, columns)
        source = weight_ref.at[:, pl.ds(sum(READY) + chunk * columns, columns)]
        copies.append(pltpu.make_async_copy(source, weight_s.at[:, part], sems.at[chunk]))
        copies[chunk].start()
    attended = jnp.concatenate([attended_ref[head] for head in range(GROUP)], axis=1)

    def projected(weight):
        return jnp.dot(attended, weight, preferred_element_type=jnp.float32).astype(jnp.bfloat16)

    start = 0
    for ready_ref in ready_refs:
        out_ref[:, start : start + ready_ref.shape[1]] = projected(ready_ref[...])
        start += ready_ref.shape[1]
    for chunk in range(chunks):
        copies[chunk].wait()
        out_ref[:, start : start + columns] = projected(weight_s[:, chunk * columns : (chunk + 1) * columns])
        start += columns


def final_kernel(
    tile_ref,
    size_ref,
    timestep_ref,
    local_ref,
    own_ref,
    other_ref,
    hidden_ref,
    mlp_ref,
    gate_ref,
    shift_ref,
    scale_ref,
    weight_ref,
    bias_ref,
    latent_ref,
    velocity_ref,
    next_ref,
    modulated_s,
):
    rows = 16
    for start in range(0, PIX, rows):
        block = slice(start, start + rows)
        projected = own_ref[block, :].astype(jnp.float32) + other_ref[block, :].astype(jnp.float32)
        state = hidden_ref[block, :].astype(jnp.float32) + gate_ref[...] * (
            projected + mlp_ref[block, :].astype(jnp.float32)
        )
        centered = state - jnp.mean(state, axis=-1, keepdims=True)
        scaled = centered * lax.rsqrt(jnp.mean(centered * centered, axis=-1, keepdims=True) + 1e-06)
        modulated_s[block, :] = (scaled * (1.0 + scale_ref[...]) + shift_ref[...]).astype(jnp.bfloat16)
    latents = weight_ref.shape[0]
    diagonal = lax.broadcasted_iota(jnp.int32, (latents, latents), 0) == lax.broadcasted_iota(
        jnp.int32, (latents, latents), 1
    )
    bias = jnp.sum(jnp.where(diagonal, bias_ref[...], 0.0), axis=1, keepdims=True)
    velocity = (
        lax.dot_general(
            weight_ref[...], modulated_s[...], (((1,), (1,)), ((), ())), preferred_element_type=jnp.float32
        )
        + bias
    )
    tile = tile_ref[0]
    tile_row = tile // GRID_X
    tile_col = tile - tile_row * GRID_X
    live = (local_ref[0:1, :] < size_ref[0] - tile_row * TILE_H) & (local_ref[1:2, :] < size_ref[1] - tile_col * TILE_W)
    velocity = jnp.where(live, velocity, 0.0)
    area = jnp.full((1, PIX), size_ref[0] * size_ref[1], jnp.int32).astype(jnp.float32)
    moment = jnp.full((1, PIX), timestep_ref[0], jnp.int32).astype(jnp.float32)
    shift_factor = jnp.exp(0.5 + 0.65 * (area - 256.0) / 3840.0)
    now_time = 1.0 - moment / STEPS
    next_time = 1.0 - (moment + 1.0) / STEPS

    def sigma_of(at):
        return shift_factor * at / (shift_factor * at + 1.0 - at)

    step = sigma_of(next_time) - sigma_of(now_time)
    velocity_ref[...] = velocity
    next_ref[...] = latent_ref[...] + step * velocity


SMEM = pl.BlockSpec(memory_space=pltpu.SMEM)
VMEM = pl.BlockSpec(memory_space=pltpu.VMEM)
HBM = pl.BlockSpec(memory_space=pltpu.HBM)


def params(mebibytes):
    return pltpu.CompilerParams(vmem_limit_bytes=mebibytes * 1024 * 1024)


def shards(
    image_qkv,
    text_kv,
    q_gain,
    k_gain,
    out_weight,
    hidden,
    mlp_term,
    gate,
    final_shift,
    final_scale,
    final_weight,
    final_bias,
    latent,
    image_size,
    text_len,
    timestep,
):
    bf16 = jnp.bfloat16
    width = GROUP * HEAD
    model = hidden.shape[2]
    latents = final_weight.shape[1]
    tile = lax.axis_index("tile").astype(jnp.int32).reshape(1)
    kind = lax.axis_index("tp").astype(jnp.int32)
    which = jnp.where(kind == 1, tile[0] // GROUP, tile[0] % GRID_X // 2)
    group = jnp.stack([2 * kind + which, 2 * kind + 1 - which])
    triple = image_qkv.reshape(PIX, 3, width).transpose(1, 0, 2)
    kinds, partners = group_tiles()
    mesh_axes = ("tile", "tp")
    groups = [[int(t) * 2 + kind for t in tiles] for kind in range(2) for tiles in kinds[kind]]
    across = [(t * 2 + kind, int(partners[kind, t]) * 2 + kind) for t in range(TILES) for kind in range(2)]

    per_step = 8
    wide = per_step * HEAD
    rope = jnp.asarray(rope_tables())

    def slab(index):
        return pl.BlockSpec((1, PIX, wide), lambda i, tile_ref: (index, 0, i))

    gain_spec = pl.BlockSpec((1, HEAD), lambda i, tile_ref: (0, 0))
    rope_spec = pl.BlockSpec((1, 2, PIX, HEAD), lambda i, tile_ref: (tile_ref[0], 0, 0, 0))
    key_value = pl.pallas_call(
        key_value_kernel,
        grid_spec=pltpu.PrefetchScalarGridSpec(
            num_scalar_prefetch=1,
            grid=(GROUP // per_step,),
            in_specs=[
                slab(1),
                slab(2),
                pl.BlockSpec((SLOTS, 2, wide), lambda i, tile_ref: (0, 0, i)),
                gain_spec,
                rope_spec,
            ],
            out_specs=pl.BlockSpec((per_step, 2 * KEYS, HEAD), lambda i, tile_ref: (i, 0, 0)),
        ),
        out_shape=jax.ShapeDtypeStruct((GROUP, 2 * KEYS, HEAD), bf16),
        name="prepare_keys",
    )(tile, triple, triple, text_kv, k_gain.reshape(1, HEAD), rope)
    own = lax.all_to_all(key_value, mesh_axes, 0, 0, axis_index_groups=groups, tiled=True)
    queries = pl.pallas_call(
        query_kernel,
        grid_spec=pltpu.PrefetchScalarGridSpec(
            num_scalar_prefetch=1,
            grid=(GROUP // per_step,),
            in_specs=[slab(0), gain_spec, rope_spec],
            out_specs=pl.BlockSpec((per_step, PIX, HEAD), lambda i, tile_ref: (i, 0, 0)),
        ),
        out_shape=jax.ShapeDtypeStruct((GROUP, PIX, HEAD), bf16),
        name="prepare_queries",
    )(tile, triple, q_gain.reshape(1, HEAD), rope)
    own, queries = lax.optimization_barrier((own, queries))
    far = lax.ppermute(own, mesh_axes, across)
    queries = lax.all_to_all(queries, mesh_axes, 0, 0, axis_index_groups=groups, tiled=True)

    queries = queries.reshape(QUERIES, HEAD)
    table = jnp.asarray(key_tables())
    acc, peak = pl.pallas_call(
        local_kernel,
        in_specs=[SMEM, SMEM, SMEM] + [VMEM] * 3,
        out_specs=(VMEM, VMEM),
        out_shape=(
            jax.ShapeDtypeStruct((QUERIES, 2 * HEAD), jnp.float32),
            jax.ShapeDtypeStruct((QUERIES, HEAD), jnp.float32),
        ),
        scratch_shapes=[pltpu.VMEM((HALF_KEYS, HEAD), bf16), pltpu.VMEM((HALF_KEYS, 2 * HEAD), bf16)],
        compiler_params=params(16),
        name="attend_local",
    )(group, image_size, text_len, table, queries, own)
    attended = pl.pallas_call(
        remote_kernel,
        in_specs=[SMEM, SMEM, SMEM] + [VMEM] * 5,
        out_specs=VMEM,
        out_shape=jax.ShapeDtypeStruct((QUERIES, HEAD), bf16),
        scratch_shapes=[pltpu.VMEM((HALF_KEYS, HEAD), bf16), pltpu.VMEM((HALF_KEYS, 2 * HEAD), bf16)],
        compiler_params=params(16),
        name="attend_far",
    )(group, image_size, text_len, table, queries, far, acc, peak)
    attended = attended.reshape(GROUP, PIX, HEAD)
    attended = lax.all_to_all(attended, mesh_axes, 0, 0, axis_index_groups=groups, tiled=True)

    ready = pl.pallas_call(
        fetch_kernel,
        in_specs=[HBM],
        out_specs=(VMEM,) * len(READY),
        out_shape=tuple(jax.ShapeDtypeStruct((width, columns), bf16) for columns in READY),
        scratch_shapes=[pltpu.SemaphoreType.DMA((len(READY),))],
        compiler_params=params(48),
        name="fetch_weight",
    )(out_weight)
    partial = pl.pallas_call(
        project_kernel,
        in_specs=[VMEM] * (1 + len(READY)) + [HBM],
        out_specs=VMEM,
        out_shape=jax.ShapeDtypeStruct((PIX, model), bf16),
        scratch_shapes=[pltpu.VMEM((width, model - sum(READY)), bf16), pltpu.SemaphoreType.DMA((2,))],
        compiler_params=params(48),
        name="project",
    )(attended, *ready, out_weight)
    other = lax.ppermute(partial, "tp", [(0, 1), (1, 0)])

    local = np.stack([np.arange(PIX) // TILE_W, np.arange(PIX) % TILE_W]).astype(np.int32)
    velocity, latent_next = pl.pallas_call(
        final_kernel,
        in_specs=[SMEM, SMEM, SMEM] + [VMEM] * 11,
        out_specs=(VMEM, VMEM),
        out_shape=(jax.ShapeDtypeStruct((latents, PIX), jnp.float32),) * 2,
        scratch_shapes=[pltpu.VMEM((PIX, model), bf16)],
        compiler_params=params(12),
        name="final_layer",
    )(
        tile,
        image_size,
        timestep,
        jnp.asarray(local),
        partial,
        other,
        hidden.reshape(PIX, model),
        mlp_term.reshape(PIX, model),
        gate.reshape(1, model),
        final_shift.reshape(1, model),
        final_scale.reshape(1, model),
        final_weight.T,
        final_bias.reshape(1, latents),
        latent.reshape(PIX, latents).T,
    )
    return (velocity.T.reshape(1, PIX, latents), latent_next.T.reshape(1, PIX, latents))


def solution(mesh):
    placed = (
        P(("req", "tile"), None, None, "tp"),
        P(("req", "tile"), None, "tp"),
        P(),
        P(),
        P("tp", None),
        P(("req", "tile"), None, None),
        P(("req", "tile"), None, None),
        P("req"),
        P("req"),
        P("req"),
        P(),
        P(),
        P(("req", "tile"), None, None),
        P("req"),
        P("req"),
        P("req"),
    )
    return jax.shard_map(
        shards,
        mesh=mesh,
        in_specs=placed,
        out_specs=(P(("req", "tile"), None, None), P(("req", "tile"), None, None)),
        check_vma=False,
    )
```

```python
import math

import jax
import jax.numpy as jnp
import numpy as np
from jax import lax
from jax.experimental import pallas as pl
from jax.experimental.pallas import tpu as pltpu
from jax.sharding import PartitionSpec as P

HEAD = 128
STEPS = 28
CANVAS = 48
TILES = 16
GRID_X = 4
TILE_H = 12
TILE_W = 12
PIX = TILE_H * TILE_W
SLOTS = 32
KEYS = PIX + SLOTS
GROUP = 8
HALF_KEYS = GROUP * KEYS
QUERIES = GROUP * PIX
QUERY_BLOCK = QUERIES // 2
FAR_BLOCK = QUERIES // 4
KEY_CHUNK = 256
READY = (1280,)
DEAD = -1e30
EXP_SCALE = HEAD ** (-0.5) * math.log2(math.e)


def position_tables():
    tile = np.arange(TILES)[:, None]
    local = np.arange(PIX)[None, :]
    row = tile // GRID_X * TILE_H + local // TILE_W
    col = tile % GRID_X * TILE_W + local % TILE_W
    return row, col


def rope_tables():
    row, col = position_tables()
    side_dims = (HEAD - HEAD // 8) // 2
    side_index = np.arange(side_dims // 2, dtype=np.float32)
    frequency = np.power(np.float32(10000.0), np.float32(-2.0) * side_index / np.float32(side_dims)).astype(np.float32)
    still = np.zeros(row.shape + (HEAD // 16,), np.float32)
    angles = np.concatenate(
        [
            still,
            row[..., None].astype(np.float32) * frequency,
            col[..., None].astype(np.float32) * frequency,
        ],
        axis=-1,
    ).astype(np.float64)
    cosine = np.repeat(np.cos(angles), 2, axis=-1)
    sine = np.repeat(np.sin(angles), 2, axis=-1)
    sine[..., 0::2] *= -1.0
    return np.stack([cosine, sine], axis=1).astype(np.float32)


def group_tiles():
    lows = np.arange(TILES // GRID_X)[:, None] * GRID_X
    kinds = [
        [(lows + np.array([0, 1])).reshape(-1), (lows + np.array([3, 2])).reshape(-1)],
        [np.arange(GROUP), np.arange(GROUP) + GROUP],
    ]
    partners = np.zeros((2, TILES), np.int64)
    for kind, (near, far) in enumerate(kinds):
        partners[kind, near] = far
        partners[kind, far] = near
    return kinds, partners


def key_tables():
    row, col = position_tables()
    far = np.full((GROUP, SLOTS), 1 << 20)
    beyond = np.full((GROUP, PIX), 1 << 20)
    tables = []
    for kind in group_tiles()[0]:
        for tiles in kind:
            slot = tiles[:, None] * SLOTS + np.arange(SLOTS)[None, :]
            parts = ((row[tiles], far), (col[tiles], far), (beyond, slot))
            tables.append(np.stack([np.concatenate(part, axis=1).reshape(HALF_KEYS) for part in parts]))
    return np.stack(tables).astype(np.int32)


def inverse_rms(vectors):
    wide = vectors.astype(jnp.float32)
    square = wide * wide
    high = square.astype(jnp.bfloat16)
    low = (square - high.astype(jnp.float32)).astype(jnp.bfloat16)
    ones = jnp.ones((2 * HEAD, HEAD), jnp.bfloat16)
    total = jnp.dot(jnp.concatenate([high, low], axis=1), ones, preferred_element_type=jnp.float32)
    return lax.rsqrt(total * (1.0 / HEAD) + 1e-06)


def swap_pairs(rows):
    even = lax.broadcasted_iota(jnp.int32, rows.shape, 1) % 2 == 0
    return jnp.where(even, pltpu.roll(rows, HEAD - 1, 1), pltpu.roll(rows, 1, 1))


def rotate_heads(source_ref, gain_ref, table_ref, out_ref):
    heads = out_ref.shape[0]
    gain = jnp.broadcast_to(gain_ref[...], (8, HEAD))
    along = table_ref[0, 0] * gain[0:1]
    across = table_ref[0, 1] * swap_pairs(gain)[0:1]
    stacked = jnp.concatenate([source_ref[0, :, h * HEAD : (h + 1) * HEAD] for h in range(heads)], axis=0)
    row = lax.broadcasted_iota(jnp.int32, (HEAD, HEAD), 0)
    col = lax.broadcasted_iota(jnp.int32, (HEAD, HEAD), 1)
    pairs = jnp.where(row + 1 - 2 * (row % 2) == col, 1.0, 0.0).astype(jnp.bfloat16)
    swapped = jnp.dot(stacked, pairs, preferred_element_type=jnp.float32)
    inverse = inverse_rms(stacked)
    for head in range(heads):
        rows = slice(head * PIX, (head + 1) * PIX)
        turned = stacked[rows].astype(jnp.float32) * along + swapped[rows] * across
        out_ref[head, 0:PIX, :] = (turned * inverse[rows]).astype(jnp.bfloat16)


def key_value_kernel(tile_ref, key_ref, value_ref, text_ref, gain_ref, table_ref, out_ref):
    rotate_heads(key_ref, gain_ref, table_ref, out_ref)
    text = text_ref[...]
    heads = out_ref.shape[0]
    text_keys = text[:, 0, :]
    text_values = text[:, 1, :]
    stacked = jnp.concatenate([text_keys[:, h * HEAD : (h + 1) * HEAD] for h in range(heads)], axis=0)
    text_keys = (stacked.astype(jnp.float32) * inverse_rms(stacked) * gain_ref[...]).astype(jnp.bfloat16)
    for head in range(heads):
        lanes = slice(head * HEAD, (head + 1) * HEAD)
        out_ref[head, PIX:KEYS, :] = text_keys[head * SLOTS : (head + 1) * SLOTS]
        out_ref[head, KEYS : KEYS + PIX, :] = value_ref[0, :, lanes]
        out_ref[head, KEYS + PIX :, :] = text_values[:, lanes]


def query_kernel(tile_ref, query_ref, gain_ref, table_ref, out_ref):
    rotate_heads(query_ref, gain_ref, table_ref, out_ref)


def key_bias(table_ref, size_ref, text_len_ref, group):
    image_ok = (table_ref[group, 0:1, :] < size_ref[0]) & (table_ref[group, 1:2, :] < size_ref[1])
    text_ok = table_ref[group, 2:3, :] < text_len_ref[0]
    return jnp.where(image_ok | text_ok, 0.0, DEAD)


def score_chunks(queries, key_s, bias):
    chunks = []
    for start in range(0, key_s.shape[0], KEY_CHUNK):
        part = slice(start, min(start + KEY_CHUNK, key_s.shape[0]))
        scores = lax.dot_general(
            queries, key_s[part, :], (((1,), (1,)), ((), ())), preferred_element_type=jnp.float32
        )
        chunks.append(scores + bias[:, part])
    return chunks


def peak_of(chunks):
    peak = jnp.max(chunks[0], axis=1, keepdims=True)
    for scores in chunks[1:]:
        peak = jnp.maximum(peak, jnp.max(scores, axis=1, keepdims=True))
    return peak


def weighted(chunks, peak, value_s):
    blended = None
    start = 0
    for scores in chunks:
        stop = start + scores.shape[1]
        weights = jnp.exp2((scores - peak) * EXP_SCALE).astype(jnp.bfloat16)
        added = jnp.dot(weights, value_s[start:stop, :], preferred_element_type=jnp.float32)
        blended = added if blended is None else blended + added
        start = stop
    return blended


def stage(source_ref, key_s, value_s):
    for tile in range(GROUP):
        rows = slice(tile * KEYS, (tile + 1) * KEYS)
        key_s[rows, :] = source_ref[tile, 0:KEYS, :]
        value_s[rows, 0:HEAD] = source_ref[tile, KEYS:, :]
    value_s[:, HEAD:] = jnp.ones((HALF_KEYS, HEAD), jnp.bfloat16)


def local_kernel(
    group_ref, size_ref, text_len_ref, table_ref, query_ref, own_ref, acc_ref, peak_ref, key_s, value_s
):
    bias = key_bias(table_ref, size_ref, text_len_ref, group_ref[0])
    stage(own_ref, key_s, value_s)
    for start in range(0, QUERIES, QUERY_BLOCK):
        block = slice(start, start + QUERY_BLOCK)
        chunks = score_chunks(query_ref[block, :], key_s, bias)
        peak = peak_of(chunks)
        acc_ref[block, :] = weighted(chunks, peak, value_s)
        peak_ref[block, :] = jnp.broadcast_to(peak, (QUERY_BLOCK, HEAD))


def remote_kernel(
    group_ref,
    size_ref,
    text_len_ref,
    table_ref,
    query_ref,
    far_ref,
    acc_ref,
    peak_ref,
    weight_ref,
    out_ref,
    ready_ref,
    key_s,
    value_s,
    sem,
):
    fetch = pltpu.make_async_copy(weight_ref.at[:, pl.ds(0, READY[0])], ready_ref, sem)
    fetch.start()
    bias = key_bias(table_ref, size_ref, text_len_ref, group_ref[1])
    stage(far_ref, key_s, value_s)
    blocks = [slice(start, start + FAR_BLOCK) for start in range(0, QUERIES, FAR_BLOCK)]
    ahead = score_chunks(query_ref[blocks[0], :], key_s, bias)
    for index, block in enumerate(blocks):
        chunks = ahead
        if index + 1 < len(blocks):
            ahead = score_chunks(query_ref[blocks[index + 1], :], key_s, bias)
        before = peak_ref[block, :]
        peak = jnp.maximum(before[:, 0:1], peak_of(chunks))
        factor = jnp.exp2((before - peak) * EXP_SCALE)
        added = weighted(chunks, peak, value_s)
        blended = acc_ref[block, 0:HEAD] * factor + added[:, 0:HEAD]
        total = acc_ref[block, HEAD:] * factor + added[:, HEAD:]
        out_ref[block, :] = (blended / total).astype(jnp.bfloat16)
    fetch.wait()


def project_kernel(attended_ref, *refs):
    ready_refs = refs[: len(READY)]
    weight_ref, out_ref, weight_s, sems = refs[len(READY) :]
    chunks = sems.shape[0]
    columns = weight_s.shape[1] // chunks
    copies = []
    for chunk in range(chunks):
        part = pl.ds(chunk * columns, columns)
        source = weight_ref.at[:, pl.ds(sum(READY) + chunk * columns, columns)]
        copies.append(pltpu.make_async_copy(source, weight_s.at[:, part], sems.at[chunk]))
        copies[chunk].start()
    attended = jnp.concatenate([attended_ref[head] for head in range(GROUP)], axis=1)

    def projected(weight):
        return jnp.dot(attended, weight, preferred_element_type=jnp.float32).astype(jnp.bfloat16)

    start = 0
    for ready_ref in ready_refs:
        out_ref[:, start : start + ready_ref.shape[1]] = projected(ready_ref[...])
        start += ready_ref.shape[1]
    for chunk in range(chunks):
        copies[chunk].wait()
        out_ref[:, start : start + columns] = projected(weight_s[:, chunk * columns : (chunk + 1) * columns])
        start += columns


def final_kernel(
    tile_ref,
    size_ref,
    timestep_ref,
    local_ref,
    own_ref,
    other_ref,
    hidden_ref,
    mlp_ref,
    gate_ref,
    shift_ref,
    scale_ref,
    weight_ref,
    bias_ref,
    latent_ref,
    velocity_ref,
    next_ref,
    modulated_s,
):
    rows = 16
    for start in range(0, PIX, rows):
        block = slice(start, start + rows)
        projected = own_ref[block, :].astype(jnp.float32) + other_ref[block, :].astype(jnp.float32)
        state = hidden_ref[block, :].astype(jnp.float32) + gate_ref[...] * (
            projected + mlp_ref[block, :].astype(jnp.float32)
        )
        centered = state - jnp.mean(state, axis=-1, keepdims=True)
        scaled = centered * lax.rsqrt(jnp.mean(centered * centered, axis=-1, keepdims=True) + 1e-06)
        modulated_s[block, :] = (scaled * (1.0 + scale_ref[...]) + shift_ref[...]).astype(jnp.bfloat16)
    latents = weight_ref.shape[0]
    diagonal = lax.broadcasted_iota(jnp.int32, (latents, latents), 0) == lax.broadcasted_iota(
        jnp.int32, (latents, latents), 1
    )
    bias = jnp.sum(jnp.where(diagonal, bias_ref[...], 0.0), axis=1, keepdims=True)
    velocity = (
        lax.dot_general(
            weight_ref[...], modulated_s[...], (((1,), (1,)), ((), ())), preferred_element_type=jnp.float32
        )
        + bias
    )
    tile = tile_ref[0]
    tile_row = tile // GRID_X
    tile_col = tile - tile_row * GRID_X
    live = (local_ref[0:1, :] < size_ref[0] - tile_row * TILE_H) & (local_ref[1:2, :] < size_ref[1] - tile_col * TILE_W)
    velocity = jnp.where(live, velocity, 0.0)
    area = jnp.full((1, PIX), size_ref[0] * size_ref[1], jnp.int32).astype(jnp.float32)
    moment = jnp.full((1, PIX), timestep_ref[0], jnp.int32).astype(jnp.float32)
    shift_factor = jnp.exp(0.5 + 0.65 * (area - 256.0) / 3840.0)
    now_time = 1.0 - moment / STEPS
    next_time = 1.0 - (moment + 1.0) / STEPS

    def sigma_of(at):
        return shift_factor * at / (shift_factor * at + 1.0 - at)

    step = sigma_of(next_time) - sigma_of(now_time)
    velocity_ref[...] = velocity
    next_ref[...] = latent_ref[...] + step * velocity


SMEM = pl.BlockSpec(memory_space=pltpu.SMEM)
VMEM = pl.BlockSpec(memory_space=pltpu.VMEM)
HBM = pl.BlockSpec(memory_space=pltpu.HBM)


def params(mebibytes):
    return pltpu.CompilerParams(vmem_limit_bytes=mebibytes * 1024 * 1024)


def shards(
    image_qkv,
    text_kv,
    q_gain,
    k_gain,
    out_weight,
    hidden,
    mlp_term,
    gate,
    final_shift,
    final_scale,
    final_weight,
    final_bias,
    latent,
    image_size,
    text_len,
    timestep,
):
    bf16 = jnp.bfloat16
    width = GROUP * HEAD
    model = hidden.shape[2]
    latents = final_weight.shape[1]
    tile = lax.axis_index("tile").astype(jnp.int32).reshape(1)
    kind = lax.axis_index("tp").astype(jnp.int32)
    which = jnp.where(kind == 1, tile[0] // GROUP, tile[0] % GRID_X // 2)
    group = jnp.stack([2 * kind + which, 2 * kind + 1 - which])
    triple = image_qkv.reshape(PIX, 3, width).transpose(1, 0, 2)
    kinds, partners = group_tiles()
    mesh_axes = ("tile", "tp")
    groups = [[int(t) * 2 + kind for t in tiles] for kind in range(2) for tiles in kinds[kind]]
    across = [(t * 2 + kind, int(partners[kind, t]) * 2 + kind) for t in range(TILES) for kind in range(2)]

    per_step = 8
    wide = per_step * HEAD
    rope = jnp.asarray(rope_tables())

    def slab(index):
        return pl.BlockSpec((1, PIX, wide), lambda i, tile_ref: (index, 0, i))

    gain_spec = pl.BlockSpec((1, HEAD), lambda i, tile_ref: (0, 0))
    rope_spec = pl.BlockSpec((1, 2, PIX, HEAD), lambda i, tile_ref: (tile_ref[0], 0, 0, 0))
    key_value = pl.pallas_call(
        key_value_kernel,
        grid_spec=pltpu.PrefetchScalarGridSpec(
            num_scalar_prefetch=1,
            grid=(GROUP // per_step,),
            in_specs=[
                slab(1),
                slab(2),
                pl.BlockSpec((SLOTS, 2, wide), lambda i, tile_ref: (0, 0, i)),
                gain_spec,
                rope_spec,
            ],
            out_specs=pl.BlockSpec((per_step, 2 * KEYS, HEAD), lambda i, tile_ref: (i, 0, 0)),
        ),
        out_shape=jax.ShapeDtypeStruct((GROUP, 2 * KEYS, HEAD), bf16),
        name="prepare_keys",
    )(tile, triple, triple, text_kv, k_gain.reshape(1, HEAD), rope)
    own = lax.all_to_all(key_value, mesh_axes, 0, 0, axis_index_groups=groups, tiled=True)
    queries = pl.pallas_call(
        query_kernel,
        grid_spec=pltpu.PrefetchScalarGridSpec(
            num_scalar_prefetch=1,
            grid=(GROUP // per_step,),
            in_specs=[slab(0), gain_spec, rope_spec],
            out_specs=pl.BlockSpec((per_step, PIX, HEAD), lambda i, tile_ref: (i, 0, 0)),
        ),
        out_shape=jax.ShapeDtypeStruct((GROUP, PIX, HEAD), bf16),
        name="prepare_queries",
    )(tile, triple, q_gain.reshape(1, HEAD), rope)
    own, queries = lax.optimization_barrier((own, queries))
    far = lax.ppermute(own, mesh_axes, across)
    queries = lax.all_to_all(queries, mesh_axes, 0, 0, axis_index_groups=groups, tiled=True)

    queries = queries.reshape(QUERIES, HEAD)
    table = jnp.asarray(key_tables())
    acc, peak = pl.pallas_call(
        local_kernel,
        in_specs=[SMEM, SMEM, SMEM] + [VMEM] * 3,
        out_specs=(VMEM, VMEM),
        out_shape=(
            jax.ShapeDtypeStruct((QUERIES, 2 * HEAD), jnp.float32),
            jax.ShapeDtypeStruct((QUERIES, HEAD), jnp.float32),
        ),
        scratch_shapes=[pltpu.VMEM((HALF_KEYS, HEAD), bf16), pltpu.VMEM((HALF_KEYS, 2 * HEAD), bf16)],
        compiler_params=params(16),
        name="attend_local",
    )(group, image_size, text_len, table, queries, own)
    attended, *ready = pl.pallas_call(
        remote_kernel,
        in_specs=[SMEM, SMEM, SMEM] + [VMEM] * 5 + [HBM],
        out_specs=(VMEM, VMEM),
        out_shape=(
            jax.ShapeDtypeStruct((QUERIES, HEAD), bf16),
            jax.ShapeDtypeStruct((width, READY[0]), bf16),
        ),
        scratch_shapes=[pltpu.VMEM((HALF_KEYS, HEAD), bf16), pltpu.VMEM((HALF_KEYS, 2 * HEAD), bf16), pltpu.SemaphoreType.DMA],
        compiler_params=params(48),
        name="attend_far",
    )(group, image_size, text_len, table, queries, far, acc, peak, out_weight)
    attended = attended.reshape(GROUP, PIX, HEAD)
    attended = lax.all_to_all(attended, mesh_axes, 0, 0, axis_index_groups=groups, tiled=True)

    partial = pl.pallas_call(
        project_kernel,
        in_specs=[VMEM] * (1 + len(READY)) + [HBM],
        out_specs=VMEM,
        out_shape=jax.ShapeDtypeStruct((PIX, model), bf16),
        scratch_shapes=[pltpu.VMEM((width, model - sum(READY)), bf16), pltpu.SemaphoreType.DMA((2,))],
        compiler_params=params(48),
        name="project",
    )(attended, *ready, out_weight)
    other = lax.ppermute(partial, "tp", [(0, 1), (1, 0)])

    local = np.stack([np.arange(PIX) // TILE_W, np.arange(PIX) % TILE_W]).astype(np.int32)
    velocity, latent_next = pl.pallas_call(
        final_kernel,
        in_specs=[SMEM, SMEM, SMEM] + [VMEM] * 11,
        out_specs=(VMEM, VMEM),
        out_shape=(jax.ShapeDtypeStruct((latents, PIX), jnp.float32),) * 2,
        scratch_shapes=[pltpu.VMEM((PIX, model), bf16)],
        compiler_params=params(12),
        name="final_layer",
    )(
        tile,
        image_size,
        timestep,
        jnp.asarray(local),
        partial,
        other,
        hidden.reshape(PIX, model),
        mlp_term.reshape(PIX, model),
        gate.reshape(1, model),
        final_shift.reshape(1, model),
        final_scale.reshape(1, model),
        final_weight.T,
        final_bias.reshape(1, latents),
        latent.reshape(PIX, latents).T,
    )
    return (velocity.T.reshape(1, PIX, latents), latent_next.T.reshape(1, PIX, latents))


def solution(mesh):
    placed = (
        P(("req", "tile"), None, None, "tp"),
        P(("req", "tile"), None, "tp"),
        P(),
        P(),
        P("tp", None),
        P(("req", "tile"), None, None),
        P(("req", "tile"), None, None),
        P("req"),
        P("req"),
        P("req"),
        P(),
        P(),
        P(("req", "tile"), None, None),
        P("req"),
        P("req"),
        P("req"),
    )
    return jax.shard_map(
        shards,
        mesh=mesh,
        in_specs=placed,
        out_specs=(P(("req", "tile"), None, None), P(("req", "tile"), None, None)),
        check_vma=False,
    )
```

```python
import math

import jax
import jax.numpy as jnp
import numpy as np
from jax import lax
from jax.experimental import pallas as pl
from jax.experimental.pallas import tpu as pltpu
from jax.sharding import PartitionSpec as P

HEAD = 128
STEPS = 28
CANVAS = 48
TILES = 16
GRID_X = 4
TILE_H = 12
TILE_W = 12
PIX = TILE_H * TILE_W
SLOTS = 32
KEYS = PIX + SLOTS
GROUP = 8
HALF_KEYS = GROUP * KEYS
QUERIES = GROUP * PIX
QUERY_BLOCK = QUERIES // 2
FAR_BLOCK = QUERIES // 4
KEY_CHUNK = 256
READY = (1280,)
DEAD = -1e30
EXP_SCALE = HEAD ** (-0.5) * math.log2(math.e)


def position_tables():
    tile = np.arange(TILES)[:, None]
    local = np.arange(PIX)[None, :]
    row = tile // GRID_X * TILE_H + local // TILE_W
    col = tile % GRID_X * TILE_W + local % TILE_W
    return row, col


def rope_tables():
    row, col = position_tables()
    side_dims = (HEAD - HEAD // 8) // 2
    side_index = np.arange(side_dims // 2, dtype=np.float32)
    frequency = np.power(np.float32(10000.0), np.float32(-2.0) * side_index / np.float32(side_dims)).astype(np.float32)
    still = np.zeros(row.shape + (HEAD // 16,), np.float32)
    angles = np.concatenate(
        [
            still,
            row[..., None].astype(np.float32) * frequency,
            col[..., None].astype(np.float32) * frequency,
        ],
        axis=-1,
    ).astype(np.float64)
    cosine = np.repeat(np.cos(angles), 2, axis=-1)
    sine = np.repeat(np.sin(angles), 2, axis=-1)
    sine[..., 0::2] *= -1.0
    return np.stack([cosine, sine], axis=1).astype(np.float32)


def group_tiles():
    lows = np.arange(TILES // GRID_X)[:, None] * GRID_X
    kinds = [
        [(lows + np.array([0, 1])).reshape(-1), (lows + np.array([3, 2])).reshape(-1)],
        [np.arange(GROUP), np.arange(GROUP) + GROUP],
    ]
    partners = np.zeros((2, TILES), np.int64)
    for kind, (near, far) in enumerate(kinds):
        partners[kind, near] = far
        partners[kind, far] = near
    return kinds, partners


def key_tables():
    row, col = position_tables()
    far = np.full((GROUP, SLOTS), 1 << 20)
    beyond = np.full((GROUP, PIX), 1 << 20)
    tables = []
    for kind in group_tiles()[0]:
        for tiles in kind:
            slot = tiles[:, None] * SLOTS + np.arange(SLOTS)[None, :]
            parts = ((row[tiles], far), (col[tiles], far), (beyond, slot))
            tables.append(np.stack([np.concatenate(part, axis=1).reshape(HALF_KEYS) for part in parts]))
    return np.stack(tables).astype(np.int32)


def inverse_rms(vectors):
    wide = vectors.astype(jnp.float32)
    square = wide * wide
    high = square.astype(jnp.bfloat16)
    low = (square - high.astype(jnp.float32)).astype(jnp.bfloat16)
    ones = jnp.ones((2 * HEAD, HEAD), jnp.bfloat16)
    total = jnp.dot(jnp.concatenate([high, low], axis=1), ones, preferred_element_type=jnp.float32)
    return lax.rsqrt(total * (1.0 / HEAD) + 1e-06)


def swap_pairs(rows):
    even = lax.broadcasted_iota(jnp.int32, rows.shape, 1) % 2 == 0
    return jnp.where(even, pltpu.roll(rows, HEAD - 1, 1), pltpu.roll(rows, 1, 1))


def rotate_heads(source_ref, gain_ref, table_ref, out_ref):
    heads = out_ref.shape[0]
    gain = jnp.broadcast_to(gain_ref[...], (8, HEAD))
    along = table_ref[0, 0] * gain[0:1]
    across = table_ref[0, 1] * swap_pairs(gain)[0:1]
    stacked = jnp.concatenate([source_ref[0, :, h * HEAD : (h + 1) * HEAD] for h in range(heads)], axis=0)
    row = lax.broadcasted_iota(jnp.int32, (HEAD, HEAD), 0)
    col = lax.broadcasted_iota(jnp.int32, (HEAD, HEAD), 1)
    pairs = jnp.where(row + 1 - 2 * (row % 2) == col, 1.0, 0.0).astype(jnp.bfloat16)
    swapped = jnp.dot(stacked, pairs, preferred_element_type=jnp.float32)
    inverse = inverse_rms(stacked)
    for head in range(heads):
        rows = slice(head * PIX, (head + 1) * PIX)
        turned = stacked[rows].astype(jnp.float32) * along + swapped[rows] * across
        out_ref[head, 0:PIX, :] = (turned * inverse[rows]).astype(jnp.bfloat16)


def key_value_kernel(tile_ref, key_ref, value_ref, text_ref, gain_ref, table_ref, out_ref):
    rotate_heads(key_ref, gain_ref, table_ref, out_ref)
    text = text_ref[...]
    heads = out_ref.shape[0]
    text_keys = text[:, 0, :]
    text_values = text[:, 1, :]
    stacked = jnp.concatenate([text_keys[:, h * HEAD : (h + 1) * HEAD] for h in range(heads)], axis=0)
    text_keys = (stacked.astype(jnp.float32) * inverse_rms(stacked) * gain_ref[...]).astype(jnp.bfloat16)
    for head in range(heads):
        lanes = slice(head * HEAD, (head + 1) * HEAD)
        out_ref[head, PIX:KEYS, :] = text_keys[head * SLOTS : (head + 1) * SLOTS]
        out_ref[head, KEYS : KEYS + PIX, :] = value_ref[0, :, lanes]
        out_ref[head, KEYS + PIX :, :] = text_values[:, lanes]


def query_kernel(tile_ref, query_ref, gain_ref, table_ref, out_ref):
    rotate_heads(query_ref, gain_ref, table_ref, out_ref)


def key_bias(table_ref, size_ref, text_len_ref, group):
    image_ok = (table_ref[group, 0:1, :] < size_ref[0]) & (table_ref[group, 1:2, :] < size_ref[1])
    text_ok = table_ref[group, 2:3, :] < text_len_ref[0]
    return jnp.where(image_ok | text_ok, 0.0, DEAD)


def score_chunks(queries, key_s, bias):
    chunks = []
    for start in range(0, key_s.shape[0], KEY_CHUNK):
        part = slice(start, min(start + KEY_CHUNK, key_s.shape[0]))
        scores = lax.dot_general(
            queries, key_s[part, :], (((1,), (1,)), ((), ())), preferred_element_type=jnp.float32
        )
        chunks.append(scores + bias[:, part])
    return chunks


def peak_of(chunks):
    peak = jnp.max(chunks[0], axis=1, keepdims=True)
    for scores in chunks[1:]:
        peak = jnp.maximum(peak, jnp.max(scores, axis=1, keepdims=True))
    return peak


def weighted(chunks, peak, value_s):
    blended = None
    start = 0
    for scores in chunks:
        stop = start + scores.shape[1]
        weights = jnp.exp2((scores - peak) * EXP_SCALE).astype(jnp.bfloat16)
        added = jnp.dot(weights, value_s[start:stop, :], preferred_element_type=jnp.float32)
        blended = added if blended is None else blended + added
        start = stop
    return blended


def stage(source_ref, key_s, value_s):
    for tile in range(GROUP):
        rows = slice(tile * KEYS, (tile + 1) * KEYS)
        key_s[rows, :] = source_ref[tile, 0:KEYS, :]
        value_s[rows, 0:HEAD] = source_ref[tile, KEYS:, :]
    value_s[:, HEAD:] = jnp.ones((HALF_KEYS, HEAD), jnp.bfloat16)


def local_kernel(
    group_ref, size_ref, text_len_ref, table_ref, query_ref, own_ref, acc_ref, peak_ref, key_s, value_s
):
    bias = key_bias(table_ref, size_ref, text_len_ref, group_ref[0])
    stage(own_ref, key_s, value_s)
    for start in range(0, QUERIES, QUERY_BLOCK):
        block = slice(start, start + QUERY_BLOCK)
        chunks = score_chunks(query_ref[block, :], key_s, bias)
        peak = peak_of(chunks)
        acc_ref[block, :] = weighted(chunks, peak, value_s)
        peak_ref[block, :] = jnp.broadcast_to(peak, (QUERY_BLOCK, HEAD))


def remote_kernel(
    group_ref,
    size_ref,
    text_len_ref,
    table_ref,
    query_ref,
    far_ref,
    acc_ref,
    peak_ref,
    weight_ref,
    out_ref,
    ready_ref,
    key_s,
    value_s,
    sem,
):
    fetch = pltpu.make_async_copy(weight_ref.at[:, pl.ds(0, READY[0])], ready_ref, sem)
    fetch.start()
    bias = key_bias(table_ref, size_ref, text_len_ref, group_ref[1])
    stage(far_ref, key_s, value_s)
    blocks = [slice(start, start + FAR_BLOCK) for start in range(0, QUERIES, FAR_BLOCK)]
    ahead = score_chunks(query_ref[blocks[0], :], key_s, bias)
    for index, block in enumerate(blocks):
        chunks = ahead
        if index + 1 < len(blocks):
            ahead = score_chunks(query_ref[blocks[index + 1], :], key_s, bias)
        before = peak_ref[block, :]
        peak = jnp.maximum(before[:, 0:1], peak_of(chunks))
        factor = jnp.exp2((before - peak) * EXP_SCALE)
        added = weighted(chunks, peak, value_s)
        blended = acc_ref[block, 0:HEAD] * factor + added[:, 0:HEAD]
        total = acc_ref[block, HEAD:] * factor + added[:, HEAD:]
        out_ref[block, :] = (blended / total).astype(jnp.bfloat16)
    fetch.wait()


def project_kernel(attended_ref, *refs):
    ready_refs = refs[: len(READY)]
    weight_ref, out_ref, weight_s, sems = refs[len(READY) :]
    chunks = sems.shape[0]
    columns = weight_s.shape[1] // chunks
    copies = []
    for chunk in range(chunks):
        part = pl.ds(chunk * columns, columns)
        source = weight_ref.at[:, pl.ds(sum(READY) + chunk * columns, columns)]
        copies.append(pltpu.make_async_copy(source, weight_s.at[:, part], sems.at[chunk]))
        copies[chunk].start()
    attended = jnp.concatenate([attended_ref[head] for head in range(GROUP)], axis=1)

    def projected(weight):
        return jnp.dot(attended, weight, preferred_element_type=jnp.float32).astype(jnp.bfloat16)

    start = 0
    for ready_ref in ready_refs:
        out_ref[:, start : start + ready_ref.shape[1]] = projected(ready_ref[...])
        start += ready_ref.shape[1]
    for chunk in range(chunks):
        copies[chunk].wait()
        out_ref[:, start : start + columns] = projected(weight_s[:, chunk * columns : (chunk + 1) * columns])
        start += columns


def final_kernel(
    tile_ref,
    size_ref,
    timestep_ref,
    local_ref,
    own_ref,
    other_ref,
    hidden_ref,
    mlp_ref,
    gate_ref,
    shift_ref,
    scale_ref,
    weight_ref,
    bias_ref,
    latent_ref,
    velocity_ref,
    next_ref,
    modulated_s,
    velocity_s,
    next_s,
    sems,
):
    rows = 16
    for start in range(0, PIX, rows):
        block = slice(start, start + rows)
        projected = own_ref[block, :].astype(jnp.float32) + other_ref[block, :].astype(jnp.float32)
        state = hidden_ref[block, :].astype(jnp.float32) + gate_ref[...] * (
            projected + mlp_ref[block, :].astype(jnp.float32)
        )
        centered = state - jnp.mean(state, axis=-1, keepdims=True)
        scaled = centered * lax.rsqrt(jnp.mean(centered * centered, axis=-1, keepdims=True) + 1e-06)
        modulated_s[block, :] = (scaled * (1.0 + scale_ref[...]) + shift_ref[...]).astype(jnp.bfloat16)
    latents = weight_ref.shape[0]
    diagonal = lax.broadcasted_iota(jnp.int32, (latents, latents), 0) == lax.broadcasted_iota(
        jnp.int32, (latents, latents), 1
    )
    bias = jnp.sum(jnp.where(diagonal, bias_ref[...], 0.0), axis=1, keepdims=True)
    velocity = (
        lax.dot_general(
            weight_ref[...], modulated_s[...], (((1,), (1,)), ((), ())), preferred_element_type=jnp.float32
        )
        + bias
    )
    tile = tile_ref[0]
    tile_row = tile // GRID_X
    tile_col = tile - tile_row * GRID_X
    live = (local_ref[0:1, :] < size_ref[0] - tile_row * TILE_H) & (local_ref[1:2, :] < size_ref[1] - tile_col * TILE_W)
    velocity = jnp.where(live, velocity, 0.0)
    velocity_s[...] = velocity
    send_velocity = pltpu.make_async_copy(velocity_s, velocity_ref, sems.at[0])
    send_velocity.start()
    area = jnp.full((1, PIX), size_ref[0] * size_ref[1], jnp.int32).astype(jnp.float32)
    moment = jnp.full((1, PIX), timestep_ref[0], jnp.int32).astype(jnp.float32)
    shift_factor = jnp.exp(0.5 + 0.65 * (area - 256.0) / 3840.0)
    now_time = 1.0 - moment / STEPS
    next_time = 1.0 - (moment + 1.0) / STEPS

    def sigma_of(at):
        return shift_factor * at / (shift_factor * at + 1.0 - at)

    step = sigma_of(next_time) - sigma_of(now_time)
    next_s[...] = latent_ref[...] + step * velocity
    send_next = pltpu.make_async_copy(next_s, next_ref, sems.at[1])
    send_next.start()
    send_velocity.wait()
    send_next.wait()


SMEM = pl.BlockSpec(memory_space=pltpu.SMEM)
VMEM = pl.BlockSpec(memory_space=pltpu.VMEM)
HBM = pl.BlockSpec(memory_space=pltpu.HBM)


def params(mebibytes):
    return pltpu.CompilerParams(vmem_limit_bytes=mebibytes * 1024 * 1024)


def shards(
    image_qkv,
    text_kv,
    q_gain,
    k_gain,
    out_weight,
    hidden,
    mlp_term,
    gate,
    final_shift,
    final_scale,
    final_weight,
    final_bias,
    latent,
    image_size,
    text_len,
    timestep,
):
    bf16 = jnp.bfloat16
    width = GROUP * HEAD
    model = hidden.shape[2]
    latents = final_weight.shape[1]
    tile = lax.axis_index("tile").astype(jnp.int32).reshape(1)
    kind = lax.axis_index("tp").astype(jnp.int32)
    which = jnp.where(kind == 1, tile[0] // GROUP, tile[0] % GRID_X // 2)
    group = jnp.stack([2 * kind + which, 2 * kind + 1 - which])
    triple = image_qkv.reshape(PIX, 3, width).transpose(1, 0, 2)
    kinds, partners = group_tiles()
    mesh_axes = ("tile", "tp")
    groups = [[int(t) * 2 + kind for t in tiles] for kind in range(2) for tiles in kinds[kind]]
    across = [(t * 2 + kind, int(partners[kind, t]) * 2 + kind) for t in range(TILES) for kind in range(2)]

    per_step = 8
    wide = per_step * HEAD
    rope = jnp.asarray(rope_tables())

    def slab(index):
        return pl.BlockSpec((1, PIX, wide), lambda i, tile_ref: (index, 0, i))

    gain_spec = pl.BlockSpec((1, HEAD), lambda i, tile_ref: (0, 0))
    rope_spec = pl.BlockSpec((1, 2, PIX, HEAD), lambda i, tile_ref: (tile_ref[0], 0, 0, 0))
    key_value = pl.pallas_call(
        key_value_kernel,
        grid_spec=pltpu.PrefetchScalarGridSpec(
            num_scalar_prefetch=1,
            grid=(GROUP // per_step,),
            in_specs=[
                slab(1),
                slab(2),
                pl.BlockSpec((SLOTS, 2, wide), lambda i, tile_ref: (0, 0, i)),
                gain_spec,
                rope_spec,
            ],
            out_specs=pl.BlockSpec((per_step, 2 * KEYS, HEAD), lambda i, tile_ref: (i, 0, 0)),
        ),
        out_shape=jax.ShapeDtypeStruct((GROUP, 2 * KEYS, HEAD), bf16),
        name="prepare_keys",
    )(tile, triple, triple, text_kv, k_gain.reshape(1, HEAD), rope)
    own = lax.all_to_all(key_value, mesh_axes, 0, 0, axis_index_groups=groups, tiled=True)
    queries = pl.pallas_call(
        query_kernel,
        grid_spec=pltpu.PrefetchScalarGridSpec(
            num_scalar_prefetch=1,
            grid=(GROUP // per_step,),
            in_specs=[slab(0), gain_spec, rope_spec],
            out_specs=pl.BlockSpec((per_step, PIX, HEAD), lambda i, tile_ref: (i, 0, 0)),
        ),
        out_shape=jax.ShapeDtypeStruct((GROUP, PIX, HEAD), bf16),
        name="prepare_queries",
    )(tile, triple, q_gain.reshape(1, HEAD), rope)
    own, queries = lax.optimization_barrier((own, queries))
    far = lax.ppermute(own, mesh_axes, across)
    queries = lax.all_to_all(queries, mesh_axes, 0, 0, axis_index_groups=groups, tiled=True)

    queries = queries.reshape(QUERIES, HEAD)
    table = jnp.asarray(key_tables())
    acc, peak = pl.pallas_call(
        local_kernel,
        in_specs=[SMEM, SMEM, SMEM] + [VMEM] * 3,
        out_specs=(VMEM, VMEM),
        out_shape=(
            jax.ShapeDtypeStruct((QUERIES, 2 * HEAD), jnp.float32),
            jax.ShapeDtypeStruct((QUERIES, HEAD), jnp.float32),
        ),
        scratch_shapes=[pltpu.VMEM((HALF_KEYS, HEAD), bf16), pltpu.VMEM((HALF_KEYS, 2 * HEAD), bf16)],
        compiler_params=params(16),
        name="attend_local",
    )(group, image_size, text_len, table, queries, own)
    attended, *ready = pl.pallas_call(
        remote_kernel,
        in_specs=[SMEM, SMEM, SMEM] + [VMEM] * 5 + [HBM],
        out_specs=(VMEM, VMEM),
        out_shape=(
            jax.ShapeDtypeStruct((QUERIES, HEAD), bf16),
            jax.ShapeDtypeStruct((width, READY[0]), bf16),
        ),
        scratch_shapes=[pltpu.VMEM((HALF_KEYS, HEAD), bf16), pltpu.VMEM((HALF_KEYS, 2 * HEAD), bf16), pltpu.SemaphoreType.DMA],
        compiler_params=params(48),
        name="attend_far",
    )(group, image_size, text_len, table, queries, far, acc, peak, out_weight)
    attended = attended.reshape(GROUP, PIX, HEAD)
    attended = lax.all_to_all(attended, mesh_axes, 0, 0, axis_index_groups=groups, tiled=True)

    partial = pl.pallas_call(
        project_kernel,
        in_specs=[VMEM] * (1 + len(READY)) + [HBM],
        out_specs=VMEM,
        out_shape=jax.ShapeDtypeStruct((PIX, model), bf16),
        scratch_shapes=[pltpu.VMEM((width, model - sum(READY)), bf16), pltpu.SemaphoreType.DMA((2,))],
        compiler_params=params(48),
        name="project",
    )(attended, *ready, out_weight)
    other = lax.ppermute(partial, "tp", [(0, 1), (1, 0)])

    local = np.stack([np.arange(PIX) // TILE_W, np.arange(PIX) % TILE_W]).astype(np.int32)
    velocity, latent_next = pl.pallas_call(
        final_kernel,
        in_specs=[SMEM, SMEM, SMEM] + [VMEM] * 11,
        out_specs=(HBM, HBM),
        out_shape=(jax.ShapeDtypeStruct((latents, PIX), jnp.float32),) * 2,
        scratch_shapes=[
            pltpu.VMEM((PIX, model), bf16),
            pltpu.VMEM((latents, PIX), jnp.float32),
            pltpu.VMEM((latents, PIX), jnp.float32),
            pltpu.SemaphoreType.DMA((2,)),
        ],
        compiler_params=params(12),
        name="final_layer",
    )(
        tile,
        image_size,
        timestep,
        jnp.asarray(local),
        partial,
        other,
        hidden.reshape(PIX, model),
        mlp_term.reshape(PIX, model),
        gate.reshape(1, model),
        final_shift.reshape(1, model),
        final_scale.reshape(1, model),
        final_weight.T,
        final_bias.reshape(1, latents),
        latent.reshape(PIX, latents).T,
    )
    return (velocity.T.reshape(1, PIX, latents), latent_next.T.reshape(1, PIX, latents))


def solution(mesh):
    placed = (
        P(("req", "tile"), None, None, "tp"),
        P(("req", "tile"), None, "tp"),
        P(),
        P(),
        P("tp", None),
        P(("req", "tile"), None, None),
        P(("req", "tile"), None, None),
        P("req"),
        P("req"),
        P("req"),
        P(),
        P(),
        P(("req", "tile"), None, None),
        P("req"),
        P("req"),
        P("req"),
    )
    return jax.shard_map(
        shards,
        mesh=mesh,
        in_specs=placed,
        out_specs=(P(("req", "tile"), None, None), P(("req", "tile"), None, None)),
        check_vma=False,
    )
```
